32 devices in a mesh: fsdp: 8 (over z, y), rep: 4 (over x, core).
Axes of the slice: x: 2, y: 2, z: 4, core: 2. Of those that a mesh axis runs over, the one named last changes fastest.
Arguments:
- block_input: bfloat16 [2, 4096, 768], P(None, ('fsdp', 'rep')), may hold values from -6 to 6
- segment_ids: int32 [2, 4096], P(None, ('fsdp', 'rep')), may hold values from -1 to 1, as said below
- out_cotangent: bfloat16 [2, 4096, 768], P(None, ('fsdp', 'rep')), may hold values from -6 to 6
- first_gain: bfloat16 [768], P('fsdp'), may hold values from 0.099609375 to 1.8984375
- first_shift: bfloat16 [768], P('fsdp'), may hold values from -3 to 3
- second_gain: bfloat16 [768], P('fsdp'), may hold values from 0.099609375 to 1.8984375
- second_shift: bfloat16 [768], P('fsdp'), may hold values from -3 to 3
- qkv_weight: bfloat16 [768, 2304], P('fsdp'), may hold values from -2 to 2
- qkv_bias: bfloat16 [2304], P('fsdp'), may hold values from -3 to 3
- proj_weight: bfloat16 [768, 768], P('fsdp'), may hold values from -0.625 to 0.625
- proj_bias: bfloat16 [768], P('fsdp'), may hold values from -3 to 3
- up_weight: bfloat16 [768, 3072], P('fsdp'), may hold values from -0.21875 to 0.21875
- up_bias: bfloat16 [3072], P('fsdp'), may hold values from -3 to 3
- down_weight: bfloat16 [3072, 768], P('fsdp'), may hold values from -0.109375 to 0.109375
- down_bias: bfloat16 [768], P('fsdp'), may hold values from -3 to 3
Outputs:
- block_output: bfloat16 [2, 4096, 768], P(None, ('fsdp', 'rep'))
- input_grad: bfloat16 [2, 4096, 768], P(None, ('fsdp', 'rep'))
- first_gain_grad: float32 [768], P('fsdp')
- first_shift_grad: float32 [768], P('fsdp')
- second_gain_grad: float32 [768], P('fsdp')
- second_shift_grad: float32 [768], P('fsdp')
- qkv_weight_grad: float32 [768, 2304], P('fsdp')
- qkv_bias_grad: float32 [2304], P('fsdp')
- proj_weight_grad: float32 [768, 768], P('fsdp')
- proj_bias_grad: float32 [768], P('fsdp')
- up_weight_grad: float32 [768, 3072], P('fsdp')
- up_bias_grad: float32 [3072], P('fsdp')
- down_weight_grad: float32 [3072, 768], P('fsdp')
- down_bias_grad: float32 [768], P('fsdp')
The draws below stay inside these ranges and needn't reach their ends.
Inputs may be any that keep to these rules, and one draw needn't show every extreme that they name: `segment_ids`: in each aligned block of 128 slots (one device's slots of a micro-batch) the live slots come first, numbered 0 and then possibly 1, followed by empty slots marked -1; a block holds 32 or more live slots, and in every micro-batch some block is full.
All inputs are finite; a program needn't handle non-finite values.
Results may differ from the reference program's by a relative error of at most 0.0092.
Values may be sent and summed in bfloat16 or wider, within the bound.
No kernel may reach another device: no remote copies, remote signals or barrier semaphores. Data moves between devices by JAX's collectives and lax.ppermute only.
A program may use at most 192 MiB of HBM per device.

```python
import math
import jax
import jax.numpy as jnp
from jax import lax

D = 768
HEADS = 12
HDIM = 64
ROT = 16
FF = 3072
SLOT = 128
MICRO = 2
TOKENS_MB = 4096
N_FSDP = 8
N_REP = 4


def draw_qkv_weight(key, part):
    base = jnp.clip(jax.random.normal(key, (D, 3 * D), jnp.float32), -4.0, 4.0) * D ** (-0.5)
    return base.astype(jnp.bfloat16)


def draw_segment_ids(key, part):
    blocks = TOKENS_MB // SLOT
    key_live, key_cut, key_full = jax.random.split(key, 3)
    live_count = jax.random.randint(key_live, (MICRO, blocks), SLOT // 4, SLOT + 1)
    full_block = jax.random.randint(key_full, (MICRO, 1), 0, blocks)
    live_count = jnp.where(jnp.arange(blocks)[None, :] == full_block, SLOT, live_count)
    raw_cut = jax.random.randint(key_cut, (MICRO, blocks), 0, SLOT + 1)
    cut_point = live_count // 2 + raw_cut % (live_count - live_count // 2 + 1)
    slots = jnp.arange(SLOT)[None, None, :]
    segments = jnp.where(slots < cut_point[..., None], 0, 1)
    segments = jnp.where(slots >= live_count[..., None], -1, segments)
    return segments.reshape(MICRO, TOKENS_MB).astype(jnp.int32)


def raised(entries, stream_key, source, target, parts, factor):
    def block_of(dim):
        return (jnp.arange(entries.shape[dim]) // (entries.shape[dim] // parts)).reshape((-1,) + (1,) * (entries.ndim - 1 - dim))

    first = jax.random.permutation(stream_key, parts)[block_of(target)]
    second = (block_of(target) + parts // 2) % parts
    return jnp.where((block_of(source) == first) | (block_of(source) == second), factor * entries, entries)


def block_scale(key, shape, shards, smallest, largest):
    level, own = 1.0, jax.random.fold_in(key, 6)
    for dim, parts in shards:
        draws = jnp.exp(jax.random.uniform(jax.random.fold_in(own, dim), (parts,), jnp.float32, smallest / len(shards), largest / len(shards)))
        level = level * jnp.repeat(draws, shape[dim] // parts).reshape([-1 if axis == dim else 1 for axis in range(len(shape))])
    return level


def normal_values(rng, shape, spread, reach, pieces=(), kind=jnp.bfloat16):
    level = block_scale(rng, shape, pieces, -0.22, 0.18) if pieces else 1.0
    drawn = jax.random.normal(rng, shape, jnp.float32) * spread * level
    return jnp.minimum(jnp.maximum(drawn, -reach), reach).astype(kind)


def bell_draw_with(own_key, shape, width, limit, pieces, heavy, kind=jnp.bfloat16):
    array = width * jax.random.normal(own_key, shape, jnp.float32)
    if pieces:
        array = array * block_scale(own_key, shape, pieces, -0.22, 0.18)
    return jnp.clip(raised(array, jax.random.fold_in(own_key, 3), *heavy), -limit, limit).astype(kind)


def setup_inputs(seed: int = 0) -> dict:
    key_list = jax.random.split(jax.random.key(seed), 16)
    block_input = normal_values(key_list[0], (MICRO, TOKENS_MB, D), 1.0, 6.0, ((1, 32),))
    segment_ids = draw_segment_ids(jax.random.fold_in(key_list[15], 71), 0)
    out_cotangent = bell_draw_with(key_list[2], (MICRO, TOKENS_MB, D), 1.0, 6.0, ((1, 32),), (1, 2, 32, 2.75))
    first_gain = jnp.clip(1.0 + 0.18 * jax.random.normal(key_list[3], (D,), jnp.float32), 0.099609375, 1.8984375).astype(jnp.bfloat16)
    first_shift = normal_values(key_list[4], (D,), 0.5, 3.0, ((0, 8),))
    second_gain = jnp.clip(1.0 + 0.18 * jax.random.normal(key_list[5], (D,), jnp.float32), 0.099609375, 1.8984375).astype(jnp.bfloat16)
    second_shift = normal_values(key_list[6], (D,), 0.5, 3.0, ((0, 8),))
    qkv_weight = draw_qkv_weight(jax.random.fold_in(key_list[15], 71), 0)
    qkv_bias = normal_values(key_list[8], (3 * D,), 0.5, 3.0, ((0, 8),))
    proj_weight = normal_values(key_list[9], (D, D), (D // 8) ** -0.5, 0.625, ((0, 8),))
    proj_bias = normal_values(key_list[10], (D,), 0.5, 3.0, ((0, 8),))
    up_weight = normal_values(key_list[11], (D, FF), D ** -0.5, 0.21875, ((0, 8),))
    up_bias = normal_values(key_list[12], (FF,), 0.5, 3.0, ((0, 8),))
    down_weight = normal_values(key_list[13], (FF, D), FF ** -0.5, 0.109375, ((0, 8),))
    down_bias = normal_values(key_list[14], (D,), 0.5, 3.0, ((0, 8),))
    return dict(block_input=block_input, segment_ids=segment_ids, out_cotangent=out_cotangent, first_gain=first_gain, first_shift=first_shift, second_gain=second_gain, second_shift=second_shift, qkv_weight=qkv_weight, qkv_bias=qkv_bias, proj_weight=proj_weight, proj_bias=proj_bias, up_weight=up_weight, up_bias=up_bias, down_weight=down_weight, down_bias=down_bias)


EPSILON = 1e-05
NEG_FILL = -1e+30

def layer_norm(values, gain, shift):
    centered = values - lax.optimization_barrier(jnp.mean(values, axis=-1, keepdims=True))
    variance = lax.optimization_barrier(jnp.mean(centered * centered, axis=-1, keepdims=True))
    inverse = lax.rsqrt(variance + EPSILON)
    unit_vals = centered * inverse
    return (unit_vals * gain + shift, unit_vals, inverse)

def norm_backward(grad_normed, unit_vals, inverse, gain):
    scaled = grad_normed * gain
    through = inverse * (scaled - lax.optimization_barrier(jnp.mean(scaled, axis=-1, keepdims=True)) - unit_vals * lax.optimization_barrier(jnp.mean(scaled * unit_vals, axis=-1, keepdims=True)))
    return (through, lax.optimization_barrier(jnp.sum(grad_normed * unit_vals, axis=0)), lax.optimization_barrier(jnp.sum(grad_normed, axis=0)))

def rotate(tensor, cosine, sine, direction):
    halfway = ROT // 2
    leading = tensor[..., :halfway]
    trailing = tensor[..., halfway:ROT]
    return jnp.concatenate([leading * cosine - direction * trailing * sine, trailing * cosine + direction * leading * sine, tensor[..., ROT:]], axis=-1)

def gelu_slope(values):
    return 0.5 * (1.0 + lax.erf(values * 0.7071067811865476)) + values * jnp.exp(-0.5 * values * values) * 0.3989422804014327

def rotary_tables(segments):
    length = segments.shape[0]
    token_order = jnp.arange(length, dtype=jnp.int32)
    same_doc = segments[:, None] == segments[None, :]
    allowed = same_doc & (token_order[None, :] <= token_order[:, None])
    before = same_doc & (token_order[None, :] < token_order[:, None])
    position = lax.optimization_barrier(jnp.sum(before.astype(jnp.float32), axis=1))
    halfway = ROT // 2
    frequency = 10000.0 ** (-jnp.arange(halfway, dtype=jnp.float32) / halfway)
    angles = position[:, None] * frequency[None, :]
    return (allowed, jnp.cos(angles)[:, None, :], jnp.sin(angles)[:, None, :])

def product(pattern, first_op, second_op):
    return jnp.einsum(pattern, first_op.astype(jnp.float32), second_op.astype(jnp.float32))

def one_slab(inputs, segments, cotangent, weights):
    first_gain, first_shift, second_gain, second_shift, qkv_weight, qkv_bias, proj_weight, proj_bias, up_weight, up_bias, down_weight, down_bias = weights
    length = inputs.shape[0]
    values = inputs.astype(jnp.float32)
    allowed, cosine, sine = rotary_tables(segments)
    live_rows = (segments >= 0).astype(jnp.float32)[:, None]
    normed_a, unit_a, inverse_a = layer_norm(values, first_gain.astype(jnp.float32), first_shift.astype(jnp.float32))
    normed_a = normed_a.astype(jnp.bfloat16)
    normed_m, unit_m, inverse_m = layer_norm(values, second_gain.astype(jnp.float32), second_shift.astype(jnp.float32))
    normed_m = normed_m.astype(jnp.bfloat16)
    projected = jnp.dot(normed_a, qkv_weight, preferred_element_type=jnp.float32) + qkv_bias.astype(jnp.float32)
    query = projected[:, :D].reshape(length, HEADS, HDIM)
    keys_raw = projected[:, D:2 * D].reshape(length, HEADS, HDIM)
    values_raw = projected[:, 2 * D:].reshape(length, HEADS, HDIM)
    query_s = (rotate(query, cosine, sine, 1.0) * 0.125).astype(jnp.bfloat16)
    keys_r = rotate(keys_raw, cosine, sine, 1.0).astype(jnp.bfloat16)
    values_b = values_raw.astype(jnp.bfloat16)
    scores = jnp.where(allowed[None], product('qhd,khd->hqk', query_s, keys_r), NEG_FILL)
    highest = lax.optimization_barrier(jnp.max(scores, axis=-1, keepdims=True))
    logsum = highest + jnp.log(lax.optimization_barrier(jnp.sum(jnp.exp(scores - highest), axis=-1, keepdims=True)))
    probs_full = jnp.exp(scores - logsum)
    probs_b = probs_full.astype(jnp.bfloat16)
    context = product('hqk,khd->qhd', probs_b, values_b).reshape(length, D).astype(jnp.bfloat16)
    attended = jnp.dot(context, proj_weight, preferred_element_type=jnp.float32) + proj_bias.astype(jnp.float32)
    pre_act = jnp.dot(normed_m, up_weight, preferred_element_type=jnp.float32) + up_bias.astype(jnp.float32)
    activ = jax.nn.gelu(pre_act, approximate=False).astype(jnp.bfloat16)
    mlp_out = jnp.dot(activ, down_weight, preferred_element_type=jnp.float32) + down_bias.astype(jnp.float32)
    block_out = (live_rows * (values + attended + mlp_out)).astype(jnp.bfloat16)
    grad_out = cotangent.astype(jnp.float32) * live_rows
    grad_outb = grad_out.astype(jnp.bfloat16)
    out_bias_grad = lax.optimization_barrier(jnp.sum(grad_out, axis=0))
    proj_grad = jnp.dot(context.T, grad_outb, preferred_element_type=jnp.float32)
    down_grad = jnp.dot(activ.T, grad_outb, preferred_element_type=jnp.float32)
    grad_context = jnp.dot(grad_outb, proj_weight.T, preferred_element_type=jnp.float32)
    grad_context = grad_context.astype(jnp.bfloat16).reshape(length, HEADS, HDIM)
    grad_act = jnp.dot(grad_outb, down_weight.T, preferred_element_type=jnp.float32)
    grad_pre = grad_act * gelu_slope(pre_act)
    up_bias_grad = lax.optimization_barrier(jnp.sum(grad_pre, axis=0))
    grad_pre_b = grad_pre.astype(jnp.bfloat16)
    up_grad = jnp.dot(normed_m.T, grad_pre_b, preferred_element_type=jnp.float32)
    grad_norm_m = jnp.dot(grad_pre_b, up_weight.T, preferred_element_type=jnp.float32)
    grad_probs = product('qhd,khd->hqk', grad_context, values_b)
    grad_value = product('hqk,qhd->khd', probs_b, grad_context)
    delta = lax.optimization_barrier(jnp.sum(probs_full * grad_probs, axis=-1, keepdims=True))
    grad_sc_b = (probs_full * (grad_probs - delta)).astype(jnp.bfloat16)
    grad_query = rotate(product('hqk,khd->qhd', grad_sc_b, keys_r) * 0.125, cosine, sine, -1.0)
    grad_key = rotate(product('hqk,qhd->khd', grad_sc_b, query_s), cosine, sine, -1.0)
    grad_proj = jnp.concatenate([grad_query.reshape(length, D), grad_key.reshape(length, D), grad_value.reshape(length, D)], axis=1)
    qkv_bias_grad = lax.optimization_barrier(jnp.sum(grad_proj, axis=0))
    grad_proj_b = grad_proj.astype(jnp.bfloat16)
    qkv_grad = jnp.dot(normed_a.T, grad_proj_b, preferred_element_type=jnp.float32)
    grad_norm_a = jnp.dot(grad_proj_b, qkv_weight.T, preferred_element_type=jnp.float32)
    through_a, first_gain_grad, first_shift_grad = norm_backward(grad_norm_a, unit_a, inverse_a, first_gain.astype(jnp.float32))
    through_m, second_gain_grad, second_shift_grad = norm_backward(grad_norm_m, unit_m, inverse_m, second_gain.astype(jnp.float32))
    input_grad = (grad_out + through_a + through_m).astype(jnp.bfloat16)
    grads = (first_gain_grad, first_shift_grad, second_gain_grad, second_shift_grad, qkv_grad, qkv_bias_grad, proj_grad, out_bias_grad, up_grad, up_bias_grad, down_grad, out_bias_grad)
    return (block_out, input_grad, grads)

def reference(block_input, segment_ids, out_cotangent, first_gain, first_shift, second_gain, second_shift, qkv_weight, qkv_bias, proj_weight, proj_bias, up_weight, up_bias, down_weight, down_bias):
    weights = (first_gain, first_shift, second_gain, second_shift, qkv_weight, qkv_bias, proj_weight, proj_bias, up_weight, up_bias, down_weight, down_bias)
    slab_total = MICRO * N_FSDP * N_REP
    group_size = math.gcd(slab_total, max(1, 4096 // SLOT))
    group_count = slab_total // group_size
    inputs = block_input.reshape(group_count, group_size, SLOT, D)
    segments = segment_ids.reshape(group_count, group_size, SLOT)
    cotangents = out_cotangent.reshape(group_count, group_size, SLOT, D)
    zero_grads = tuple((jnp.zeros(weight.shape, jnp.float32) for weight in weights))

    def scan_step(carry, batch_item):
        slab_outs, slab_dx, slab_grads = jax.vmap(one_slab, in_axes=(0, 0, 0, None))(batch_item[0], batch_item[1], batch_item[2], weights)
        updated = tuple((running + lax.optimization_barrier(jnp.sum(added, axis=0)) for running, added in zip(carry, slab_grads)))
        return (updated, (slab_outs, slab_dx))
    totals, (all_outs, all_dx) = lax.scan(scan_step, zero_grads, (inputs, segments, cotangents))
    return (all_outs.reshape(block_input.shape), all_dx.reshape(block_input.shape), totals[0], totals[1], totals[2], totals[3], totals[4], totals[5], totals[6], totals[7], totals[8], totals[9], totals[10], totals[11])
```

```python
import jax
import jax.numpy as jnp
from jax import lax
from jax.sharding import PartitionSpec as P

D = 768
HEADS = 12
HDIM = 64
ROT = 16
FF = 3072
CORES = 2
HALF = D // CORES
LOCAL_HEADS = HEADS // CORES
VEC_LANES = 128

EPSILON = 1e-05
NEG_FILL = -1e30
BF16 = jnp.bfloat16
F32 = jnp.float32


def dot(left, right):
    return jnp.dot(left, right, preferred_element_type=F32)


def dot_t(left, right):
    return lax.dot_general(left, right, (((1,), (1,)), ((), ())), preferred_element_type=F32)


def t_dot(left, right):
    return lax.dot_general(left, right, (((0,), (0,)), ((), ())), preferred_element_type=F32)


def rotate(tensor, cosine, sine, direction):
    halfway = ROT // 2
    leading = tensor[..., :halfway]
    trailing = tensor[..., halfway:ROT]
    return jnp.concatenate(
        [
            leading * cosine - direction * trailing * sine,
            trailing * cosine + direction * leading * sine,
            tensor[..., ROT:],
        ],
        axis=-1,
    )


def rotary_tables(segments):
    length = segments.shape[0]
    token_order = jnp.arange(length, dtype=jnp.int32)
    same_doc = segments[:, None] == segments[None, :]
    allowed = same_doc & (token_order[None, :] <= token_order[:, None])
    before = same_doc & (token_order[None, :] < token_order[:, None])
    position = jnp.sum(before.astype(F32), axis=1)
    halfway = ROT // 2
    frequency = 10000.0 ** (-jnp.arange(halfway, dtype=F32) / halfway)
    angles = position[:, None] * frequency[None, :]
    return (allowed, jnp.cos(angles)[:, None, :], jnp.sin(angles)[:, None, :])


def attention(slab_proj, grad_context, segments):
    length = slab_proj.shape[0]
    allowed, cosine, sine = rotary_tables(segments)
    query = slab_proj[:, :HALF].reshape(length, LOCAL_HEADS, HDIM)
    keys_raw = slab_proj[:, HALF : 2 * HALF].reshape(length, LOCAL_HEADS, HDIM)
    values_b = slab_proj[:, 2 * HALF :].reshape(length, LOCAL_HEADS, HDIM).astype(BF16)
    query_s = (rotate(query, cosine, sine, 1.0) * 0.125).astype(BF16)
    keys_r = rotate(keys_raw, cosine, sine, 1.0).astype(BF16)
    grad_context = grad_context.reshape(length, LOCAL_HEADS, HDIM)
    scores = jnp.einsum("qhd,khd->hqk", query_s, keys_r, preferred_element_type=F32)
    scores = jnp.where(allowed[None], scores, NEG_FILL)
    highest = jnp.max(scores, axis=-1, keepdims=True)
    logsum = highest + jnp.log(jnp.sum(jnp.exp(scores - highest), axis=-1, keepdims=True))
    probs = jnp.exp(scores - logsum)
    probs_b = probs.astype(BF16)
    context = jnp.einsum("hqk,khd->qhd", probs_b, values_b, preferred_element_type=F32)
    context = context.reshape(length, HALF).astype(BF16)
    grad_probs = jnp.einsum("qhd,khd->hqk", grad_context, values_b, preferred_element_type=F32)
    grad_value = jnp.einsum("hqk,qhd->khd", probs_b, grad_context, preferred_element_type=F32)
    delta = jnp.sum(probs * grad_probs, axis=-1, keepdims=True)
    grad_sc = (probs * (grad_probs - delta)).astype(BF16)
    grad_query = jnp.einsum("hqk,khd->qhd", grad_sc, keys_r, preferred_element_type=F32)
    grad_query = rotate(grad_query * 0.125, cosine, sine, -1.0)
    grad_key = jnp.einsum("hqk,qhd->khd", grad_sc, query_s, preferred_element_type=F32)
    grad_key = rotate(grad_key, cosine, sine, -1.0)
    grad_proj = jnp.concatenate(
        [
            grad_query.reshape(length, HALF),
            grad_key.reshape(length, HALF),
            grad_value.reshape(length, HALF),
        ],
        axis=1,
    )
    return context, grad_proj


def gelu_slope(values):
    return (
        0.5 * (1.0 + lax.erf(values * 0.7071067811865476))
        + values * jnp.exp(-0.5 * values * values) * 0.3989422804014327
    )


def make_body(shards):
    bits = shards.bit_length() - 1
    rows = D // shards
    lowest_first = [1 << k for k in range(bits)]
    highest_first = lowest_first[::-1]

    def reverse(value, width):
        return sum(((value >> k) & 1) << (width - 1 - k) for k in range(width))

    def shard_swap(value, mask):
        return lax.ppermute(value, "fsdp", [(i, i ^ mask) for i in range(shards)])

    def core_swap(value):
        return lax.ppermute(value, "rep", [(i, i ^ 1) for i in range(4)])

    def x_swap(value):
        return lax.ppermute(value, "rep", [(i, i ^ 2) for i in range(4)])

    def gather_all(own):
        for mask in highest_first:
            own = jnp.concatenate([own, shard_swap(own, mask)], axis=0)
        return own

    def reduce_all(part):
        for mask in lowest_first:
            half = part.shape[0] // 2
            sent = shard_swap(part[half:].astype(BF16), mask)
            part = part[:half] + sent.astype(F32)
        return part

    def body(
        block_input,
        segment_ids,
        out_cotangent,
        first_gain,
        first_shift,
        second_gain,
        second_shift,
        qkv_weight,
        qkv_bias,
        proj_weight,
        proj_bias,
        up_weight,
        up_bias,
        down_weight,
        down_bias,
    ):
        micro, slot = block_input.shape[0], block_input.shape[1]
        own_tokens = micro * slot
        tokens = CORES * own_tokens
        mine = lax.axis_index("fsdp")
        rep = lax.axis_index("rep")
        core = rep % 2
        across = rep // 2
        top = mine // (shards // 2)

        up_own = lax.dynamic_index_in_dim(
            up_weight.reshape(rows, shards, 4, rows), rep, axis=2, keepdims=False
        ).reshape(rows, D)
        down_own = lax.dynamic_index_in_dim(
            down_weight.reshape(4, rows, D), rep, axis=0, keepdims=False
        )
        qkv_own = lax.dynamic_index_in_dim(
            qkv_weight.reshape(rows, 3, CORES, HALF), core, axis=2, keepdims=False
        ).reshape(rows, 3 * HALF)
        vector_own = jnp.concatenate(
            [
                jnp.stack([first_gain, first_shift, second_gain, second_shift], axis=0),
                qkv_bias.reshape(3, rows),
                proj_bias[None],
                up_bias.reshape(4, rows),
                down_bias[None],
            ],
            axis=0,
        )
        vector_own = jnp.pad(vector_own, ((0, VEC_LANES - 13), (0, 0))).T

        segment_row = jnp.pad(
            segment_ids.reshape(1, own_tokens).astype(BF16), ((0, 15), (0, D - own_tokens))
        )
        token_pack = jnp.concatenate(
            [block_input.reshape(own_tokens, D), out_cotangent.reshape(own_tokens, D), segment_row], axis=0
        )
        token_other = core_swap(token_pack)

        up_first = gather_all(up_own)
        down_first = gather_all(down_own)
        up_second = x_swap(up_first)
        down_second = x_swap(down_first)

        column_part = jnp.concatenate([qkv_own, vector_own], axis=1)
        column_width = column_part.shape[1]
        mask = highest_first[0]
        received = shard_swap(jnp.concatenate([column_part, proj_weight], axis=1), mask)
        proj_block = jnp.where(top == core, proj_weight, received[:, column_width:])
        packed = jnp.concatenate(
            [
                jnp.concatenate([column_part, received[:, :column_width]], axis=0),
                jnp.concatenate([proj_block[:, :HALF], proj_block[:, HALF:]], axis=0),
            ],
            axis=1,
        )
        for mask in highest_first[1:]:
            packed = jnp.concatenate([packed, shard_swap(packed, mask)], axis=0)
        qkv_rel = packed[:, : 3 * HALF]
        vector_rel = packed[:, 3 * HALF : column_width].T
        proj_split = packed[:, column_width:].reshape(shards // 2, 2, rows, HALF)
        proj_left = proj_split[:, 0].reshape(HALF, HALF)
        proj_right = proj_split[:, 1].reshape(HALF, HALF)

        place = jnp.array([reverse(p, bits) for p in range(shards)], jnp.int32)
        natural = ((place ^ mine)[:, None] * rows + jnp.arange(rows)[None, :]).reshape(1, D)
        to_rel = (jnp.arange(D)[:, None] == natural).astype(BF16)
        low_place = jnp.array([reverse(p, bits - 1) << 0 for p in range(shards // 2)], jnp.int32)
        low_mine = mine % (shards // 2)
        low_natural = ((low_place ^ low_mine)[:, None] * rows + jnp.arange(rows)[None, :]).reshape(1, HALF)
        head_to_rel = (jnp.arange(HALF)[:, None] == low_natural).astype(BF16)

        vectors = vector_rel[:16].astype(BF16)
        vectors_nat = dot_t(vectors, to_rel)
        vectors = vectors.astype(F32)
        gain_a, shift_a, gain_m, shift_m = (vectors[k][None] for k in range(4))
        qkv_bias_nat = vectors_nat[4:7].reshape(3, shards, rows).transpose(1, 0, 2).reshape(3, CORES, HALF)
        qkv_bias_nat = lax.dynamic_index_in_dim(qkv_bias_nat, core, axis=1, keepdims=False).reshape(1, 3 * HALF)
        up_bias_rel = vectors[8:12]
        out_bias = (vectors_nat[7] + vectors_nat[12])[None]

        both = jnp.concatenate(
            [token_pack[:own_tokens], token_other[:own_tokens]], axis=0
        )
        segments = jnp.stack([token_pack[2 * own_tokens, :own_tokens], token_other[2 * own_tokens, :own_tokens]])
        segments = segments.astype(jnp.int32).reshape(CORES * micro, slot)
        live = (segments.reshape(tokens, 1) >= 0).astype(F32)
        cotangent = jnp.concatenate(
            [token_pack[own_tokens : 2 * own_tokens], token_other[own_tokens : 2 * own_tokens]], axis=0
        )
        grad_out = (cotangent.astype(F32) * live).astype(BF16)

        values = dot(both, to_rel)
        centered = values - jnp.mean(values, axis=-1, keepdims=True)
        variance = jnp.mean(centered * centered, axis=-1, keepdims=True)
        inverse = lax.rsqrt(variance + EPSILON)
        unit = centered * inverse
        normed_a = (unit * gain_a + shift_a).astype(BF16)
        normed_m = (unit * gain_m + shift_m).astype(BF16)

        def mlp_forward(up_nat, quarter):
            up_rel = dot(up_nat, to_rel).astype(BF16)
            bias = lax.dynamic_index_in_dim(up_bias_rel, quarter, axis=0)
            pre_act = dot(normed_m, up_rel) + bias
            activ = jax.nn.gelu(pre_act, approximate=False).astype(BF16)
            return up_rel, pre_act, activ

        def mlp_backward(up_rel, pre_act, down):
            grad_pre = dot_t(grad_out, down) * gelu_slope(pre_act)
            bias_grad = jnp.sum(grad_pre, axis=0)
            grad_pre_b = grad_pre.astype(BF16)
            grad_norm = dot_t(grad_pre_b, up_rel)
            up_grad = t_dot(normed_m, dot_t(grad_pre_b, to_rel).astype(BF16))
            return bias_grad, grad_norm, up_grad

        other = rep ^ 2
        up_rel_1, pre_1, activ_1 = mlp_forward(up_first, rep)
        up_rel_2, pre_2, activ_2 = mlp_forward(up_second, other)
        down_sent = x_swap(t_dot(activ_2, grad_out).astype(BF16))
        down_grad = t_dot(activ_1, grad_out) + down_sent.astype(F32)
        down_grad = reduce_all(down_grad)

        bias_2, grad_norm_2, up_grad_2 = mlp_backward(up_rel_2, pre_2, down_second)
        up_sent = x_swap(up_grad_2.astype(BF16))
        bias_1, grad_norm_1, up_grad_1 = mlp_backward(up_rel_1, pre_1, down_first)
        up_grad = reduce_all(up_grad_1 + up_sent.astype(F32))
        grad_norm_m = grad_norm_1 + grad_norm_2

        projected = dot(normed_a, qkv_rel) + qkv_bias_nat
        grad_context = (
            dot_t(grad_out[:, :HALF], proj_left) + dot_t(grad_out[:, HALF:], proj_right)
        ).astype(BF16)
        grad_context = dot_t(grad_context, head_to_rel).astype(BF16)
        context, grad_proj = jax.vmap(attention)(
            projected.reshape(CORES * micro, slot, 3 * HALF),
            grad_context.reshape(CORES * micro, slot, HALF),
            segments,
        )
        context = context.reshape(tokens, HALF)
        grad_proj = grad_proj.reshape(tokens, 3 * HALF)
        context_rel = dot(context, head_to_rel).astype(BF16)
        qkv_bias_grad = jnp.sum(grad_proj, axis=0)
        grad_proj_b = grad_proj.astype(BF16)
        grad_norm_a = dot_t(grad_proj_b, qkv_rel)
        qkv_grad = t_dot(normed_a, grad_proj_b)
        proj_grad = jnp.stack(
            [
                t_dot(context_rel, grad_out[:, :HALF]).reshape(shards // 2, rows, HALF),
                t_dot(context_rel, grad_out[:, HALF:]).reshape(shards // 2, rows, HALF),
            ],
            axis=1,
        ).reshape(D, HALF)

        attended = jnp.concatenate([dot(context_rel, proj_left), dot(context_rel, proj_right)], axis=1)
        out_part = attended + dot(activ_1, down_first) + dot(activ_2, down_second)
        mixed = grad_norm_a * gain_a + grad_norm_m * gain_m
        swapped = core_swap(jnp.concatenate([out_part[own_tokens:], mixed[own_tokens:]], axis=1))
        own_live = live[:own_tokens]
        block_out = own_live * (
            both[:own_tokens].astype(F32) + out_part[:own_tokens] + swapped[:, :D] + out_bias
        )
        error = mixed[:own_tokens] + swapped[:, D:]
        own_unit = unit[:own_tokens]
        through = inverse[:own_tokens] * (
            error
            - jnp.mean(error, axis=-1, keepdims=True)
            - own_unit * jnp.mean(error * own_unit, axis=-1, keepdims=True)
        )
        grad_out_rel = dot(grad_out[:own_tokens], to_rel)
        input_grad = dot_t((grad_out_rel + through).astype(BF16), to_rel).astype(BF16)

        out_bias_grad = jnp.sum(grad_out[:own_tokens].astype(F32), axis=0)
        qkv_bias_all = jnp.where(
            (jnp.arange(CORES) == core)[None, :, None], qkv_bias_grad.reshape(3, 1, HALF), 0.0
        )
        qkv_bias_all = qkv_bias_all.reshape(shards, 3, rows).transpose(1, 0, 2).reshape(3, D)
        natural_grads = jnp.concatenate([qkv_bias_all, out_bias_grad[None]], axis=0).astype(BF16)
        quarter = jnp.arange(4)[:, None]
        up_bias_grad = jnp.where(quarter == rep, bias_1[None], 0.0) + jnp.where(quarter == other, bias_2[None], 0.0)
        vector_grads = jnp.concatenate(
            [
                jnp.sum(grad_norm_a * unit, axis=0)[None],
                jnp.sum(grad_norm_a, axis=0)[None],
                jnp.sum(grad_norm_m * unit, axis=0)[None],
                jnp.sum(grad_norm_m, axis=0)[None],
                dot(natural_grads, to_rel),
                up_bias_grad,
            ],
            axis=0,
        )
        vector_grads = jnp.pad(vector_grads, ((0, VEC_LANES - 12), (0, 0))).T

        grads = jnp.concatenate([qkv_grad, vector_grads, proj_grad], axis=1)
        for mask in lowest_first[:-1]:
            half = grads.shape[0] // 2
            sent = shard_swap(grads[half:].astype(BF16), mask)
            grads = grads[:half] + sent.astype(F32)
        column_grads = grads[:, :column_width]
        proj_block = jnp.concatenate([grads[:rows, column_width:], grads[rows:, column_width:]], axis=1)
        sent = jnp.concatenate([column_grads[rows:], proj_block], axis=1).astype(BF16)
        sent = shard_swap(sent, lowest_first[-1]).astype(F32)
        column_grads = column_grads[:rows] + sent[:, :column_width]
        proj_block = proj_block + sent[:, column_width:]

        shared = jnp.concatenate([column_grads, proj_block, down_grad, up_grad], axis=1).astype(BF16)
        crossed = x_swap(shared)
        summed = column_grads.shape[1] + D
        total = (shared[:, :summed].astype(F32) + crossed[:, :summed].astype(F32)).astype(BF16)
        mine_all = jnp.concatenate([total, shared[:, summed:], crossed[:, summed:]], axis=1)
        other_all = core_swap(mine_all)

        first, second = (
            jnp.where(core == 0, mine_all, other_all),
            jnp.where(core == 0, other_all, mine_all),
        )
        qkv_out = jnp.stack(
            [first[:, : 3 * HALF].reshape(rows, 3, HALF), second[:, : 3 * HALF].reshape(rows, 3, HALF)], axis=2
        ).reshape(rows, 3 * D)
        vec_out = (
            mine_all[:, 3 * HALF : column_width].astype(F32) + other_all[:, 3 * HALF : column_width].astype(F32)
        ).T
        proj_out = jnp.where(top == 0, first[:, column_width:summed], second[:, column_width:summed])

        def quarters(start):
            pieces = []
            for side in range(2):
                for each in (first, second):
                    own = each[:, summed + start : summed + start + D]
                    far = each[:, summed + 2 * D + start : summed + 2 * D + start + D]
                    pieces.append(jnp.where(across == side, own, far))
            return pieces

        down_out = jnp.concatenate(quarters(0), axis=0)
        up_out = jnp.stack([piece.reshape(rows, shards, rows) for piece in quarters(D)], axis=2).reshape(rows, FF)
        out_vec = vec_out[7]
        return (
            block_out.astype(BF16).reshape(micro, slot, D),
            input_grad.reshape(micro, slot, D),
            vec_out[0],
            vec_out[1],
            vec_out[2],
            vec_out[3],
            qkv_out.astype(F32),
            vec_out[4:7].reshape(3 * rows),
            proj_out.astype(F32),
            out_vec,
            up_out.astype(F32),
            vec_out[8:12].reshape(4 * rows),
            down_out.astype(F32),
            out_vec,
        )

    return body


def solution(mesh):
    in_specs = (
        P(None, ("fsdp", "rep"), None),
        P(None, ("fsdp", "rep")),
        P(None, ("fsdp", "rep"), None),
        P("fsdp"),
        P("fsdp"),
        P("fsdp"),
        P("fsdp"),
        P("fsdp", None),
        P("fsdp"),
        P("fsdp", None),
        P("fsdp"),
        P("fsdp", None),
        P("fsdp"),
        P("fsdp", None),
        P("fsdp"),
    )
    out_specs = (
        P(None, ("fsdp", "rep"), None),
        P(None, ("fsdp", "rep"), None),
        P("fsdp"),
        P("fsdp"),
        P("fsdp"),
        P("fsdp"),
        P("fsdp", None),
        P("fsdp"),
        P("fsdp", None),
        P("fsdp"),
        P("fsdp", None),
        P("fsdp"),
        P("fsdp", None),
        P("fsdp"),
    )
    return jax.shard_map(
        make_body(mesh.shape["fsdp"]), mesh=mesh, in_specs=in_specs, out_specs=out_specs, check_vma=False
    )
```

```python
import functools

import jax
import jax.numpy as jnp
import numpy as np
from jax import lax
from jax.experimental import pallas as pl
from jax.experimental.pallas import tpu as pltpu
from jax.sharding import PartitionSpec as P


D = 768
HEADS = 12
HDIM = 64
ROT = 16
FF = 3072
GROUP = 4
QUART = D // GROUP
LOCAL_HEADS = HEADS // GROUP
VEC_LANES = 128

EPSILON = 1e-05
NEG_FILL = -1e30
BF16 = jnp.bfloat16
F32 = jnp.float32


def dot(left, right):
    return jnp.dot(left, right, preferred_element_type=F32)


def dot_t(left, right):
    return lax.dot_general(left, right, (((1,), (1,)), ((), ())), preferred_element_type=F32)


def t_dot(left, right):
    return lax.dot_general(left, right, (((0,), (0,)), ((), ())), preferred_element_type=F32)


LANES = 128
EXT = LOCAL_HEADS * LANES


def layer_norm(values, gain_a, shift_a):
    centered = values - jnp.mean(values, axis=-1, keepdims=True)
    variance = jnp.mean(centered * centered, axis=-1, keepdims=True)
    inverse = lax.rsqrt(variance + EPSILON)
    unit = centered * inverse
    return (unit * gain_a + shift_a).astype(BF16), unit


def take(step, refs, rows):
    value = refs[-1][rows]
    for place in range(len(refs) - 2, -1, -1):
        value = jnp.where(step == place, refs[place][rows], value)
    return value


def mlp_kernel(
    near, across, beside, far, up_lo, up_hi, down_lo, down_hi, to_rel, rep,
    keep, send, out_part, grad_norm, vectors_out, sums,
    up_rel, down_rel, down_acc, up_acc,
):
    step = pl.program_id(0)
    packs = (near, across, beside, far)
    own = (near.shape[0] - 16) // 2
    half = D // 2

    @pl.when(step == 0)
    def _():
        up_rel[:half] = dot(up_lo[:, :D], to_rel[...]).astype(BF16)
        up_rel[half:] = dot(up_hi[:, :D], to_rel[...]).astype(BF16)
        down_rel[:half] = down_lo[...]
        down_rel[half:] = down_hi[...]
        vectors_out[:, :half] = up_lo[:, D:].astype(F32).T[:16]
        vectors_out[:, half:] = up_hi[:, D:].astype(F32).T[:16]
        down_acc[...] = jnp.zeros_like(down_acc)
        up_acc[...] = jnp.zeros_like(up_acc)
        sums[...] = jnp.zeros_like(sums)

    inputs = take(step, packs, slice(0, own))
    grad_out = take(step, packs, slice(own, 2 * own))
    normed, unit = layer_norm(dot(inputs, to_rel[...]), vectors_out[2:3], vectors_out[3:4])
    bias = vectors_out[11:12]
    for quarter in range(GROUP - 1):
        bias = jnp.where(rep[0] == quarter, vectors_out[8 + quarter : 9 + quarter], bias)
    pre_act = dot(normed, up_rel[...]) + bias
    phi = 0.5 * (1.0 + lax.erf(pre_act * 0.7071067811865476))
    activ = (pre_act * phi).astype(BF16)
    slope = phi + pre_act * jnp.exp(-0.5 * pre_act * pre_act) * 0.3989422804014327
    down_acc[...] += t_dot(activ, grad_out)
    grad_pre = dot_t(grad_out, down_rel[...]) * slope
    grad_pre_b = grad_pre.astype(BF16)
    grad_nat = dot_t(grad_pre_b, to_rel[...]).astype(BF16)
    up_acc[...] += t_dot(normed, grad_nat)
    gn = dot_t(grad_pre_b, up_rel[...])
    out_part[0] = dot(activ, down_rel[...])
    grad_norm[0] = gn
    sums[0:1] += jnp.sum(gn * unit, axis=0, keepdims=True)
    sums[1:2] += jnp.sum(gn, axis=0, keepdims=True)
    sums[2:3] += jnp.sum(grad_pre, axis=0, keepdims=True)

    @pl.when(step == pl.num_programs(0) - 1)
    def _():
        keep[:, :D] = down_acc[:half].astype(BF16)
        send[:, :D] = down_acc[half:].astype(BF16)
        keep[:, D:] = up_acc[:half].astype(BF16)
        send[:, D:] = up_acc[half:].astype(BF16)


def attention_kernel(
    block_rows,
    near, across, beside, far, qkv_lo, qkv_hi, proj, to_rel, vectors, mlp_sums, place, spread, head_spread,
    cosines, sines, mlp_part, mlp_norm, rep,
    keep, send, partial_near, partial_far,
    wide, proj_wide, bias_wide, qkv_acc, proj_acc, gp_ref, ctx_ref, sums, bias_sums,
):
    step = pl.program_id(0)
    packs = (near, across, beside, far)
    half = D // 2
    own = (near.shape[0] - 16) // 2
    count = 2 * own

    @pl.when(step == 0)
    def _():
        wide[:half] = dot(qkv_lo[...], spread[...]).astype(BF16)
        wide[half:] = dot(qkv_hi[...], spread[...]).astype(BF16)
        proj_wide[...] = dot(head_spread[...], proj[...]).astype(BF16)
        vectors_b = vectors[...].astype(BF16)
        bias = sum(dot_t(vectors_b[4 + k : 5 + k], place[:, k * D : (k + 1) * D]) for k in range(3))
        bias = jnp.broadcast_to(bias, (8, bias.shape[1])).astype(BF16)
        bias_wide[...] = dot(bias, spread[...])
        qkv_acc[...] = jnp.zeros_like(qkv_acc)
        proj_acc[...] = jnp.zeros_like(proj_acc)
        sums[...] = jnp.zeros_like(sums)
        bias_sums[...] = jnp.zeros_like(bias_sums)

    inputs = take(step, packs, slice(0, own))
    grad_out = take(step, packs, slice(own, count))
    segment_row = take(step, packs, slice(count, count + 16)).astype(F32)
    normed, unit = layer_norm(dot(inputs, to_rel[...]), vectors[0:1], vectors[1:2])
    projected = dot(normed, wide[...]) + bias_wide[0:1]
    grad_context = dot_t(grad_out, proj_wide[...]).astype(BF16)
    lane = lax.broadcasted_iota(jnp.int32, (LANES, LANES), 1)
    sublane = lax.broadcasted_iota(jnp.int32, (LANES, LANES), 0)
    lower = lane < HDIM
    zero = jnp.zeros((LANES, LANES), F32)
    for slab in range(own // LANES):
        row = slice(slab * LANES, (slab + 1) * LANES)
        seg_keys = jnp.broadcast_to(segment_row[0:1, row], (LANES, LANES))
        seg_queries = seg_keys.T
        same = seg_keys == seg_queries
        allowed = same & (lane <= sublane)
        position = jnp.sum(jnp.where(same & (lane < sublane), 1.0, 0.0), axis=1, keepdims=True)
        pick = (lane.astype(F32) == position).astype(BF16)
        cos = dot(pick, cosines[0]) + dot(pick, cosines[1]) + dot(pick, cosines[2])
        sin = dot(pick, sines[0]) + dot(pick, sines[1]) + dot(pick, sines[2])

        def turn(value, direction):
            return value * cos + direction * (pltpu.roll(value, HDIM, 1) * sin)

        for head in range(LOCAL_HEADS):
            def part(which):
                start = which * EXT + head * LANES
                return slice(start, start + LANES)

            query = (turn(projected[row, part(0)], 1.0) * 0.125).astype(BF16)
            key = turn(projected[row, part(1)], 1.0).astype(BF16)
            value = projected[row, part(2)].astype(BF16)
            gctx = grad_context[row, part(0)]
            query_half = jnp.where(lower, query, jnp.zeros_like(query))
            scores = jnp.where(allowed, dot_t(query_half, key), NEG_FILL)
            highest = jnp.max(scores, axis=-1, keepdims=True)
            weight = jnp.exp(scores - highest)
            probs = weight / jnp.sum(weight, axis=-1, keepdims=True)
            probs_b = probs.astype(BF16)
            ctx_ref[row, part(0)] = dot(probs_b, value).astype(BF16)
            grad_probs = dot_t(gctx, value)
            grad_value = t_dot(probs_b, gctx)
            delta = jnp.sum(probs * grad_probs, axis=-1, keepdims=True)
            grad_sc = (probs * (grad_probs - delta)).astype(BF16)
            grad_query = jnp.where(lower, turn(dot(grad_sc, key) * 0.125, -1.0), zero)
            grad_key = jnp.where(lower, turn(t_dot(grad_sc, query), -1.0), zero)
            for which, grad in enumerate((grad_query, grad_key, grad_value)):
                gp_ref[row, part(which)] = grad.astype(BF16)
                bias_sums[0:1, part(which)] += jnp.sum(grad, axis=0, keepdims=True)

    grad_wide = gp_ref[...]
    qkv_acc[...] += t_dot(normed, dot_t(grad_wide, spread[...]).astype(BF16))
    gn = dot_t(grad_wide, wide[...])
    context = ctx_ref[...]
    proj_acc[...] += t_dot(dot(context, head_spread[...]).astype(BF16), grad_out)
    out_part = (dot(context, proj_wide[...]) + mlp_part[0]).astype(BF16)
    mixed = (gn * vectors[0:1] + mlp_norm[0] * vectors[2:3]).astype(BF16)
    sums[0:1] += jnp.sum(gn * unit, axis=0, keepdims=True)
    sums[1:2] += jnp.sum(gn, axis=0, keepdims=True)

    @pl.when(step < 2)
    def _():
        partial_near[0, :, :D] = out_part
        partial_near[0, :, D:] = mixed

    @pl.when(step >= 2)
    def _():
        partial_far[0, :, :D] = out_part
        partial_far[0, :, D:] = mixed

    @pl.when(step == 0)
    def _():
        sums[2:3] = jnp.sum(grad_out.astype(F32), axis=0, keepdims=True)

    @pl.when(step == pl.num_programs(0) - 1)
    def _():
        width = 3 * QUART
        side = width + VEC_LANES
        vec = lax.broadcasted_iota(jnp.int32, (VEC_LANES, D), 0)
        out_bias = dot(sums[...].astype(BF16), to_rel[...])[2:3]
        small = dot_t(bias_sums[...].astype(BF16), spread[...]).astype(BF16)
        small = dot(small, place[...])
        rows = [sums[0:1], sums[1:2], mlp_sums[0:1], mlp_sums[1:2]]
        rows += [small[0:1, k * D : (k + 1) * D] for k in range(3)] + [out_bias]
        table = jnp.where(vec == 8 + rep[0], mlp_sums[2:3], 0.0)
        for index, line in enumerate(rows):
            table = jnp.where(vec == index, line, table)
        table = table.T.astype(BF16)
        keep[:, :width] = qkv_acc[:half].astype(BF16)
        send[:, :width] = qkv_acc[half:].astype(BF16)
        keep[:, width:side] = table[:half]
        send[:, width:side] = table[half:]
        for target, first in ((keep, 0), (send, QUART // 2)):
            piece = proj_acc[first : first + QUART // 2]
            block = min(block_rows, QUART // 2)
            for start in range(0, QUART // 2, block):
                for quarter in range(GROUP):
                    target[
                        start * GROUP + quarter * block : start * GROUP + (quarter + 1) * block, side:
                    ] = piece[start : start + block, quarter * QUART : (quarter + 1) * QUART].astype(BF16)


def whole(*shape):
    return pl.BlockSpec(shape, lambda i: (0,) * len(shape))


def token_block(count, width):
    return pl.BlockSpec((1, count, width), lambda i: (i, 0, 0))


PARAMS = pltpu.CompilerParams(vmem_limit_bytes=60 * 1024 * 1024)


def smem():
    return pl.BlockSpec(memory_space=pltpu.SMEM)


def run_mlp(packs, up_lo, up_hi, down_lo, down_hi, to_rel, rep):
    packed = packs[0].shape[0]
    own = (packed - 16) // 2
    half = D // 2
    wide = D + VEC_LANES
    grad = jax.ShapeDtypeStruct((half, 2 * D), BF16)
    acts = jax.ShapeDtypeStruct((GROUP, own, D), F32)
    return pl.pallas_call(
        mlp_kernel,
        grid=(GROUP,),
        in_specs=[whole(packed, D)] * 4
        + [whole(half, wide), whole(half, wide), whole(half, D), whole(half, D), whole(D, D), smem()],
        out_specs=[whole(half, 2 * D)] * 2 + [token_block(own, D)] * 2 + [whole(16, D), whole(8, D)],
        out_shape=[grad] * 2 + [acts] * 2 + [jax.ShapeDtypeStruct((16, D), F32), jax.ShapeDtypeStruct((8, D), F32)],
        scratch_shapes=[
            pltpu.VMEM((D, D), BF16),
            pltpu.VMEM((D, D), BF16),
            pltpu.VMEM((D, D), F32),
            pltpu.VMEM((D, D), F32),
        ],
        compiler_params=PARAMS,
        name="mlp",
    )(*packs, up_lo, up_hi, down_lo, down_hi, to_rel, rep)


def run_attention(packs, qkv_lo, qkv_hi, proj, to_rel, vectors, mlp_sums, place, head_spread, mlp_part, mlp_norm, rep, rows):
    packed = packs[0].shape[0]
    own = (packed - 16) // 2
    half = D // 2
    width = 3 * QUART
    column = np.arange(3 * EXT)
    which, head, unit = column // EXT, column % EXT // LANES, column % LANES
    inner = unit % HDIM
    halfway = ROT // 2
    partner = np.where(inner < halfway, inner + halfway, np.where(inner < ROT, inner - halfway, inner))
    source = which * QUART + head * HDIM + np.where(unit < HDIM, inner, partner)
    source = np.where((which == 2) & (unit >= HDIM), -1, source)
    spread = (jnp.arange(width)[:, None] == jnp.asarray(source, jnp.int32)[None, :]).astype(BF16)
    lane = np.arange(LANES) % HDIM
    angle = np.arange(LANES)[:, None] * (10000.0 ** (-(lane % halfway) / halfway))[None, :]
    sign = np.where(lane < halfway, -1.0, 1.0) * np.where(np.arange(LANES) < HDIM, 1.0, -1.0)
    turning = (lane < ROT)[None, :]
    tables = []
    for table in (np.where(turning, np.cos(angle), 1.0), np.where(turning, np.sin(angle) * sign, 0.0)):
        left = table.astype(np.float32)
        pieces = []
        for _ in range(3):
            piece = left.astype(BF16)
            pieces.append(piece)
            left = left - piece.astype(np.float32)
        tables.append(jnp.asarray(np.stack(pieces)))
    total = width + VEC_LANES + QUART
    grad = jax.ShapeDtypeStruct((half, total), BF16)
    part = jax.ShapeDtypeStruct((2, own, 2 * D), BF16)
    return pl.pallas_call(
        functools.partial(attention_kernel, rows),
        grid=(GROUP,),
        in_specs=[whole(packed, D)] * 4
        + [
            whole(half, width),
            whole(half, width),
            whole(QUART, D),
            whole(D, D),
            whole(16, D),
            whole(8, D),
            whole(width, 3 * D),
            whole(width, 3 * EXT),
            whole(EXT, QUART),
            whole(3, LANES, LANES),
            whole(3, LANES, LANES),
            token_block(own, D),
            token_block(own, D),
            smem(),
        ],
        out_specs=[
            whole(half, total),
            whole(half, total),
            pl.BlockSpec((1, own, 2 * D), lambda i: (jnp.minimum(i, 1), 0, 0)),
            pl.BlockSpec((1, own, 2 * D), lambda i: (jnp.maximum(i - 2, 0), 0, 0)),
        ],
        out_shape=[grad, grad, part, part],
        scratch_shapes=[
            pltpu.VMEM((D, 3 * EXT), BF16),
            pltpu.VMEM((EXT, D), BF16),
            pltpu.VMEM((8, 3 * EXT), F32),
            pltpu.VMEM((D, width), F32),
            pltpu.VMEM((QUART, D), F32),
            pltpu.VMEM((own, 3 * EXT), BF16),
            pltpu.VMEM((own, EXT), BF16),
            pltpu.VMEM((8, D), F32),
            pltpu.VMEM((8, 3 * EXT), F32),
        ],
        compiler_params=PARAMS,
        name="attention",
    )(
        *packs, qkv_lo, qkv_hi, proj, to_rel, vectors, mlp_sums, place, spread, head_spread, *tables, mlp_part, mlp_norm, rep
    )


def finish_kernel(pack, near, received, to_rel, out_bias, live, block_out, input_grad):
    own = near.shape[0]
    partial = near[...].astype(F32) + received[...].astype(F32)
    block_out[...] = (live[...] * (pack[:own].astype(F32) + partial[:, :D] + out_bias[...])).astype(BF16)
    values = dot(pack[:own], to_rel[...])
    centered = values - jnp.mean(values, axis=-1, keepdims=True)
    inverse = lax.rsqrt(jnp.mean(centered * centered, axis=-1, keepdims=True) + EPSILON)
    unit = centered * inverse
    error = partial[:, D:]
    through = inverse * (
        error
        - jnp.mean(error, axis=-1, keepdims=True)
        - unit * jnp.mean(error * unit, axis=-1, keepdims=True)
    )
    grad = (dot(pack[own : 2 * own], to_rel[...]) + through).astype(BF16)
    input_grad[...] = dot_t(grad, to_rel[...]).astype(BF16)


def run_finish(pack, near, received, to_rel, out_bias, live):
    own = near.shape[0]
    out = jax.ShapeDtypeStruct((own, D), BF16)
    return pl.pallas_call(finish_kernel, out_shape=[out, out], compiler_params=PARAMS, name="finish")(
        pack, near, received, to_rel, out_bias, live
    )


def assemble_kernel(*refs):
    pairs, columns = refs[:4], refs[4:8]
    place = refs[8]
    qkv_out, proj_out, up_out, down_out, vec_out = refs[9:]
    rows = proj_out.shape[0]
    width = 3 * QUART
    side = width + VEC_LANES
    rep, top = place[0], place[1]

    def owner(values, natural):
        first, second, third, fourth = values
        chosen = jnp.where(rep == natural ^ 1, third, fourth)
        chosen = jnp.where(rep == natural ^ 2, second, chosen)
        return jnp.where(rep == natural, first, chosen)

    for natural in range(GROUP):
        down_out[natural * rows : (natural + 1) * rows] = owner([ref[:, :D].astype(F32) for ref in pairs], natural)
        up = owner([ref[:, D:].astype(F32) for ref in pairs], natural)
        for shard in range(D // rows):
            start = (shard * GROUP + natural) * rows
            up_out[:, start : start + rows] = up[:, shard * rows : (shard + 1) * rows]
        qkv = owner([ref[:, :width].astype(F32) for ref in columns], natural)
        for which in range(3):
            start = (which * GROUP + natural) * QUART
            qkv_out[:, start : start + QUART] = qkv[:, which * QUART : (which + 1) * QUART]
    parts = [ref[:, side:].astype(F32) for ref in columns]
    chosen = jnp.where((rep ^ top) == 1, parts[2], parts[3])
    chosen = jnp.where((rep ^ top) == 2, parts[1], chosen)
    proj_out[...] = jnp.where((rep ^ top) == 0, parts[0], chosen)
    vec = [ref[:, width:side].astype(F32) for ref in columns]
    vec_out[...] = ((vec[0] + vec[1]) + (vec[2] + vec[3])).T[:16]


def run_assemble(pairs, columns, place, rows):
    shapes = [(rows, 3 * D), (rows, D), (rows, FF), (GROUP * rows, D), (16, rows)]
    return pl.pallas_call(
        assemble_kernel,
        in_specs=[pl.BlockSpec(memory_space=pltpu.VMEM)] * 8 + [smem()],
        out_shape=[jax.ShapeDtypeStruct(shape, F32) for shape in shapes],
        compiler_params=PARAMS,
        name="assemble",
    )(*pairs, *columns, place)


def assemble_plain(pairs, columns, place, rows):
    width = 3 * QUART
    side = width + VEC_LANES
    rep, top = place[0], place[1]
    pairs = jnp.stack(pairs).astype(F32)
    columns = jnp.stack(columns).astype(F32)
    natural = jnp.arange(GROUP)
    swapped = natural ^ rep
    order = (swapped % 2) * 2 + swapped // 2
    pairs_nat, columns_nat = pairs[order], columns[order]
    qkv = columns_nat[:, :, :width].reshape(GROUP, rows, 3, QUART).transpose(1, 2, 0, 3)
    up = pairs_nat[:, :, D:].reshape(GROUP, rows, D // rows, rows).transpose(1, 2, 0, 3)
    vec = columns[:, :, width:side]
    vec = ((vec[0] + vec[1]) + (vec[2] + vec[3])).T[:16]
    return (
        qkv.reshape(rows, 3 * D),
        columns_nat[top][:, side:],
        up.reshape(rows, FF),
        pairs_nat[:, :, :D].reshape(GROUP * rows, D),
        vec,
    )


def quarter_kernel(up, qkv, vectors, rep, up_own, qkv_own):
    rows = up.shape[0]
    for natural in range(GROUP):

        @pl.when(rep[0] == natural)
        def _():
            for shard in range(D // rows):
                start = (shard * GROUP + natural) * rows
                up_own[:, shard * rows : (shard + 1) * rows] = up[:, start : start + rows]
            for which in range(3):
                start = (which * GROUP + natural) * QUART
                qkv_own[:, which * QUART : (which + 1) * QUART] = qkv[:, start : start + QUART]

    up_own[:, D:] = jnp.pad(vectors[...], ((0, VEC_LANES - 16), (0, 0))).T.astype(BF16)


def run_quarter(up, qkv, vectors, rep):
    rows = up.shape[0]
    return pl.pallas_call(
        quarter_kernel,
        in_specs=[pl.BlockSpec(memory_space=pltpu.VMEM)] * 3 + [smem()],
        out_shape=[
            jax.ShapeDtypeStruct((rows, D + VEC_LANES), BF16),
            jax.ShapeDtypeStruct((rows, 3 * QUART), BF16),
        ],
        compiler_params=PARAMS,
        name="quarter",
    )(up, qkv, vectors, rep)


def make_body(shards):
    bits = shards.bit_length() - 1
    rows = D // shards
    lowest_first = [1 << k for k in range(bits)]
    highest_first = lowest_first[::-1]

    def reverse(value, width):
        return sum(((value >> k) & 1) << (width - 1 - k) for k in range(width))

    def shard_swap(value, mask):
        return lax.ppermute(value, "fsdp", [(i, i ^ mask) for i in range(shards)])

    def core_swap(value):
        return lax.ppermute(value, "rep", [(i, i ^ 1) for i in range(GROUP)])

    def x_swap(value):
        return lax.ppermute(value, "rep", [(i, i ^ 2) for i in range(GROUP)])

    def gather_all(own):
        for mask in highest_first[:-1]:
            own = jnp.concatenate([own, shard_swap(own, mask)], axis=0)
        return own, shard_swap(own, highest_first[-1])

    def add(keep, received):
        return keep.astype(F32) + received.astype(F32)

    def reduce_all(keep, send):
        for mask in lowest_first:
            total = add(keep, shard_swap(send, mask)).astype(BF16)
            half = total.shape[0] // 2
            keep, send = total[:half], total[half:]
        return total

    def one_hot(count, width, mine):
        place = jnp.array([reverse(p, width) for p in range(count)], jnp.int32)
        natural = ((place ^ mine)[:, None] * rows + jnp.arange(rows)[None, :]).reshape(1, count * rows)
        return (jnp.arange(count * rows)[:, None] == natural).astype(BF16)

    def body(
        block_input,
        segment_ids,
        out_cotangent,
        first_gain,
        first_shift,
        second_gain,
        second_shift,
        qkv_weight,
        qkv_bias,
        proj_weight,
        proj_bias,
        up_weight,
        up_bias,
        down_weight,
        down_bias,
    ):
        micro, slot = block_input.shape[0], block_input.shape[1]
        own_tokens = micro * slot
        mine = lax.axis_index("fsdp")
        rep = lax.axis_index("rep")
        core = rep % 2
        across = rep // 2
        top = mine // (shards // 4)
        top_across, top_core = top // 2, top % 2

        rep_ref = rep.reshape(1)
        vector_own = jnp.concatenate(
            [first_gain, first_shift, second_gain, second_shift, qkv_bias, proj_bias, up_bias, down_bias]
        )
        vector_own = jnp.pad(vector_own.reshape(13, rows), ((0, 3), (0, 0)))
        if rows % 32:
            up_own = lax.dynamic_index_in_dim(
                up_weight.reshape(rows, shards, GROUP, rows), rep, axis=2, keepdims=False
            ).reshape(rows, D)
            up_own = jnp.concatenate([up_own, jnp.pad(vector_own, ((0, VEC_LANES - 16), (0, 0))).T], axis=1)
            qkv_own = lax.dynamic_index_in_dim(
                qkv_weight.reshape(rows, 3, GROUP, QUART), rep, axis=2, keepdims=False
            ).reshape(rows, 3 * QUART)
        else:
            up_own, qkv_own = run_quarter(up_weight, qkv_weight, vector_own.astype(F32), rep_ref)
        down_own = lax.dynamic_index_in_dim(
            down_weight.reshape(GROUP, rows, D), rep, axis=0, keepdims=False
        )

        live = (segment_ids.reshape(own_tokens, 1) >= 0).astype(F32)
        own_input = block_input.reshape(own_tokens, D)
        own_grad = (out_cotangent.reshape(own_tokens, D).astype(F32) * live).astype(BF16)
        segment_row = jnp.pad(
            segment_ids.reshape(1, own_tokens).astype(BF16), ((0, 15), (0, D - own_tokens))
        )
        token_pack = jnp.concatenate([own_input, own_grad, segment_row], axis=0)
        token_across = x_swap(token_pack)
        token_beside = core_swap(token_pack)
        token_far = core_swap(token_across)
        packs = (token_pack, token_across, token_beside, token_far)

        up_lo, up_hi = gather_all(up_own)
        down_lo, down_hi = gather_all(down_own)
        qkv_lo, qkv_hi = gather_all(qkv_own)

        proj_part = jnp.where(top_across == across, proj_weight, shard_swap(proj_weight, highest_first[0]))
        proj_part = jnp.where(top_core == core, proj_part, shard_swap(proj_part, highest_first[1]))
        for mask in highest_first[2:]:
            proj_part = jnp.concatenate([proj_part, shard_swap(proj_part, mask)], axis=0)

        to_rel = one_hot(shards, bits, mine)
        head_to_rel = one_hot(shards // 4, bits - 2, mine % (shards // 4))
        head_spread = jnp.pad(
            head_to_rel.reshape(LOCAL_HEADS, HDIM, QUART), ((0, 0), (0, LANES - HDIM), (0, 0))
        ).reshape(EXT, QUART)

        width = 3 * QUART
        place = jnp.array([reverse(p, bits) for p in range(shards)], jnp.int32)
        shard_start = (place ^ mine)[None, :, None] * (3 * rows)
        found = shard_start + jnp.arange(3)[:, None, None] * rows + jnp.arange(rows)[None, None, :]
        found = found.reshape(1, 3 * D)
        found = jnp.where(found % D // QUART == rep, found // D * QUART + found % QUART, -1)
        bias_place = (jnp.arange(width)[:, None] == found).astype(BF16)

        keep, send, mlp_part, mlp_norm, vectors, mlp_sums = run_mlp(
            packs, up_lo, up_hi, down_lo, down_hi, to_rel, rep_ref
        )
        pair = reduce_all(keep, send)
        keep, send, partial, partial_far = run_attention(
            packs, qkv_lo, qkv_hi, proj_part, to_rel, vectors, mlp_sums, bias_place, head_spread,
            mlp_part, mlp_norm, rep_ref, rows,
        )

        side = width + VEC_LANES
        for mask in lowest_first[:-2]:
            total = add(keep, shard_swap(send, mask)).astype(BF16)
            half = total.shape[0] // 2
            keep, send = total[:half], total[half:]
        columns, proj_block = total[:, :side], total[:, side:]
        proj_block = jnp.concatenate([proj_block[: 2 * rows], proj_block[2 * rows :]], axis=1)
        packed = jnp.concatenate([columns[2 * rows :], proj_block], axis=1)
        sent = shard_swap(packed, lowest_first[-2])
        columns = add(columns[: 2 * rows], sent[:, :side])
        proj_block = add(proj_block, sent[:, side:])
        proj_block = jnp.concatenate(
            [
                proj_block[:rows, :QUART],
                proj_block[rows:, :QUART],
                proj_block[:rows, QUART:],
                proj_block[rows:, QUART:],
            ],
            axis=1,
        ).astype(BF16)
        packed = jnp.concatenate([columns[rows:].astype(BF16), proj_block], axis=1)
        own = jnp.concatenate([columns[:rows].astype(BF16), proj_block], axis=1)
        column = add(own, shard_swap(packed, lowest_first[-1])).astype(BF16)

        summed = add(partial, core_swap(partial_far))
        received = x_swap(summed[1].astype(BF16))
        vectors_nat = dot_t(vectors.astype(BF16), to_rel)
        out_bias = (vectors_nat[7] + vectors_nat[12])[None]
        block_out, input_grad = run_finish(token_pack, summed[0], received, to_rel, out_bias, live)

        pair_across = x_swap(pair)
        pair_all = (pair, pair_across, core_swap(pair), core_swap(pair_across))
        column_across = x_swap(column)
        column_all = (column, column_across, core_swap(column), core_swap(column_across))
        assemble = assemble_plain if rows % 32 else run_assemble
        qkv_out, proj_out, up_out, down_out, vec_out = assemble(
            pair_all, column_all, jnp.stack([rep, top]), rows
        )
        return (
            block_out.reshape(micro, slot, D),
            input_grad.reshape(micro, slot, D),
            vec_out[0],
            vec_out[1],
            vec_out[2],
            vec_out[3],
            qkv_out,
            vec_out[4:7].reshape(3 * rows),
            proj_out,
            vec_out[7],
            up_out,
            vec_out[8:12].reshape(GROUP * rows),
            down_out,
            vec_out[7],
        )

    return body


def solution(mesh):
    in_specs = (
        P(None, ("fsdp", "rep"), None),
        P(None, ("fsdp", "rep")),
        P(None, ("fsdp", "rep"), None),
        P("fsdp"),
        P("fsdp"),
        P("fsdp"),
        P("fsdp"),
        P("fsdp", None),
        P("fsdp"),
        P("fsdp", None),
        P("fsdp"),
        P("fsdp", None),
        P("fsdp"),
        P("fsdp", None),
        P("fsdp"),
    )
    out_specs = (
        P(None, ("fsdp", "rep"), None),
        P(None, ("fsdp", "rep"), None),
        P("fsdp"),
        P("fsdp"),
        P("fsdp"),
        P("fsdp"),
        P("fsdp", None),
        P("fsdp"),
        P("fsdp", None),
        P("fsdp"),
        P("fsdp", None),
        P("fsdp"),
        P("fsdp", None),
        P("fsdp"),
    )
    plain = make_body(mesh.shape["fsdp"])

    return jax.shard_map(plain, mesh=mesh, in_specs=in_specs, out_specs=out_specs, check_vma=False)
```

```python
import functools

import jax
import jax.numpy as jnp
import numpy as np
from jax import lax
from jax.experimental import pallas as pl
from jax.experimental.pallas import tpu as pltpu
from jax.sharding import PartitionSpec as P


D = 768
HEADS = 12
HDIM = 64
ROT = 16
FF = 3072
GROUP = 4
QUART = D // GROUP
LOCAL_HEADS = HEADS // GROUP
VEC_LANES = 128

EPSILON = 1e-05
NEG_FILL = -1e30
BF16 = jnp.bfloat16
F32 = jnp.float32


def dot(left, right):
    return jnp.dot(left, right, preferred_element_type=F32)


def dot_t(left, right):
    return lax.dot_general(left, right, (((1,), (1,)), ((), ())), preferred_element_type=F32)


def t_dot(left, right):
    return lax.dot_general(left, right, (((0,), (0,)), ((), ())), preferred_element_type=F32)


LANES = 128
EXT = LOCAL_HEADS * LANES


def layer_norm(values, gain_a, shift_a):
    centered = values - jnp.mean(values, axis=-1, keepdims=True)
    variance = jnp.mean(centered * centered, axis=-1, keepdims=True)
    inverse = lax.rsqrt(variance + EPSILON)
    unit = centered * inverse
    return (unit * gain_a + shift_a).astype(BF16), unit


def take(step, refs, rows):
    value = refs[-1][rows]
    for place in range(len(refs) - 2, -1, -1):
        value = jnp.where(step == place, refs[place][rows], value)
    return value


def mlp_kernel(
    down_place,
    near, across, beside, far, up_lo, up_hi, down_lo, down_hi, to_rel, rep,
    keep, send, out_part, grad_norm, values_out, vectors_out, sums,
    up_rel, down_rel, down_acc, up_acc,
):
    step = pl.program_id(0)
    packs = (near, across, beside, far)
    own = (near.shape[0] - 16) // 2
    half = D // 2

    @pl.when(step == 0)
    def _():
        up_rel[:half] = dot(up_lo[:, :D], to_rel[...]).astype(BF16)
        up_rel[half:] = dot(up_hi[:, :D], to_rel[...]).astype(BF16)
        block = D // len(down_place)
        if down_place == sorted(down_place):
            down_rel[:half] = down_lo[...]
            down_rel[half:] = down_hi[...]
        else:
            for source, target in enumerate(down_place):
                piece = down_hi if source * block >= half else down_lo
                start = source * block % half
                down_rel[target * block : (target + 1) * block] = piece[start : start + block]
        vectors_out[:, :half] = up_lo[:, D:].astype(F32).T[:16]
        vectors_out[:, half:] = up_hi[:, D:].astype(F32).T[:16]
        down_acc[...] = jnp.zeros_like(down_acc)
        up_acc[...] = jnp.zeros_like(up_acc)
        sums[...] = jnp.zeros_like(sums)

    inputs = take(step, packs, slice(0, own))
    grad_out = take(step, packs, slice(own, 2 * own))
    values = dot(inputs, to_rel[...])
    values_out[0] = values.astype(BF16)
    normed, unit = layer_norm(values, vectors_out[2:3], vectors_out[3:4])
    bias = vectors_out[11:12]
    for quarter in range(GROUP - 1):
        bias = jnp.where(rep[0] == quarter, vectors_out[8 + quarter : 9 + quarter], bias)
    pre_act = dot(normed, up_rel[...]) + bias
    phi = 0.5 * (1.0 + lax.erf(pre_act * 0.7071067811865476))
    activ = (pre_act * phi).astype(BF16)
    slope = phi + pre_act * jnp.exp(-0.5 * pre_act * pre_act) * 0.3989422804014327
    down_acc[...] += t_dot(activ, grad_out)
    grad_pre = dot_t(grad_out, down_rel[...]) * slope
    grad_pre_b = grad_pre.astype(BF16)
    up_acc[...] += t_dot(normed, grad_pre_b)
    gn = dot_t(grad_pre_b, up_rel[...])
    out_part[0] = dot(activ, down_rel[...])
    grad_norm[0] = gn
    sums[0:1] += jnp.sum(gn * unit, axis=0, keepdims=True)
    sums[1:2] += jnp.sum(gn, axis=0, keepdims=True)
    sums[2:3] += jnp.sum(grad_pre, axis=0, keepdims=True)

    @pl.when(step == pl.num_programs(0) - 1)
    def _():
        keep[:, :D] = down_acc[:half].astype(BF16)
        send[:, :D] = down_acc[half:].astype(BF16)
        keep[:, D:] = dot_t(up_acc[:half].astype(BF16), to_rel[...]).astype(BF16)
        send[:, D:] = dot_t(up_acc[half:].astype(BF16), to_rel[...]).astype(BF16)


def attention_kernel(
    block_rows,
    near, across, beside, far, qkv_lo, qkv_hi, proj, to_rel, vectors, mlp_sums, place, spread, head_spread,
    cosines, sines, mlp_part, mlp_norm, values, rep,
    keep, send, partial_near, partial_far,
    wide, proj_wide, bias_wide, qkv_rel, qkv_acc, proj_acc, gp_ref, ctx_ref, sums, bias_sums,
):
    step = pl.program_id(0)
    packs = (near, across, beside, far)
    half = D // 2
    own = (near.shape[0] - 16) // 2
    count = 2 * own

    @pl.when(step == 0)
    def _():
        qkv_rel[:half] = qkv_lo[...]
        qkv_rel[half:] = qkv_hi[...]
        wide[:half] = dot(qkv_lo[...], spread[...]).astype(BF16)
        wide[half:] = dot(qkv_hi[...], spread[...]).astype(BF16)
        proj_wide[...] = dot(head_spread[...], proj[...]).astype(BF16)
        vectors_b = vectors[...].astype(BF16)
        bias = sum(dot_t(vectors_b[4 + k : 5 + k], place[:, k * D : (k + 1) * D]) for k in range(3))
        bias = jnp.broadcast_to(bias, (8, bias.shape[1])).astype(BF16)
        bias_wide[...] = dot(bias, spread[...])
        qkv_acc[...] = jnp.zeros_like(qkv_acc)
        proj_acc[...] = jnp.zeros_like(proj_acc)
        sums[...] = jnp.zeros_like(sums)
        bias_sums[...] = jnp.zeros_like(bias_sums)

    grad_out = take(step, packs, slice(own, count))
    segment_row = take(step, packs, slice(count, count + 16)).astype(F32)
    normed, unit = layer_norm(values[0].astype(F32), vectors[0:1], vectors[1:2])
    projected = dot(normed, wide[...]) + bias_wide[0:1]
    grad_context = dot_t(grad_out, proj_wide[...]).astype(BF16)
    lane = lax.broadcasted_iota(jnp.int32, (LANES, LANES), 1)
    sublane = lax.broadcasted_iota(jnp.int32, (LANES, LANES), 0)
    lower = lane < HDIM
    units = [(slab, head) for slab in range(own // LANES) for head in range(LOCAL_HEADS)]
    allowed, cos, sin = [], [], []
    for slab in range(own // LANES):
        seg_keys = jnp.broadcast_to(segment_row[0:1, slab * LANES : (slab + 1) * LANES], (LANES, LANES))
        same = seg_keys == seg_keys.T
        allowed.append(same & (lane <= sublane))
        position = jnp.sum(jnp.where(same & (lane < sublane), 1.0, 0.0), axis=1, keepdims=True)
        pick = (lane.astype(F32) == position).astype(BF16)
        cos.append(dot(pick, cosines[0]) + dot(pick, cosines[1]) + dot(pick, cosines[2]))
        sin.append(dot(pick, sines[0]) + dot(pick, sines[1]) + dot(pick, sines[2]))

    def part(value, unit, which):
        slab, head = unit
        start = which * EXT + head * LANES
        return value[slab * LANES : (slab + 1) * LANES, start : start + LANES]

    def turn(value, slab, direction):
        return value * cos[slab] + direction * (pltpu.roll(value, HDIM, 1) * sin[slab])

    query = [(turn(part(projected, u, 0), u[0], 1.0) * 0.125).astype(BF16) for u in units]
    key = [turn(part(projected, u, 1), u[0], 1.0).astype(BF16) for u in units]
    value = [part(projected, u, 2).astype(BF16) for u in units]
    gctx = [part(grad_context, u, 0) for u in units]
    count = range(len(units))
    scores = [dot_t(jnp.where(lower, query[n], jnp.zeros_like(query[n])), key[n]) for n in count]
    grad_probs = [dot_t(gctx[n], value[n]) for n in count]
    scores = [jnp.where(allowed[units[n][0]], scores[n], NEG_FILL) for n in count]
    weight = [jnp.exp(score - jnp.max(score, axis=-1, keepdims=True)) for score in scores]
    probs = [each * (1.0 / jnp.sum(each, axis=-1, keepdims=True)) for each in weight]
    probs_b = [each.astype(BF16) for each in probs]
    context = [dot(probs_b[n], value[n]) for n in count]
    grad_value = [t_dot(probs_b[n], gctx[n]) for n in count]
    delta = [jnp.sum(probs[n] * grad_probs[n], axis=-1, keepdims=True) for n in count]
    grad_sc = [(probs[n] * (grad_probs[n] - delta[n])).astype(BF16) for n in count]
    grad_query = [dot(grad_sc[n], key[n]) for n in count]
    grad_key = [t_dot(grad_sc[n], query[n]) for n in count]
    for n, (slab, head) in enumerate(units):
        row = slice(slab * LANES, (slab + 1) * LANES)
        ctx_ref[row, head * LANES : (head + 1) * LANES] = context[n].astype(BF16)
        turned = (
            turn(grad_query[n] * 0.125, slab, -1.0),
            turn(grad_key[n], slab, -1.0),
            grad_value[n],
        )
        for which, grad in enumerate(turned):
            start = which * QUART + head * HDIM
            gp_ref[row, start : start + HDIM] = grad[:, :HDIM]

    grad_proj = gp_ref[...]
    bias_sums[0:1] += jnp.sum(grad_proj, axis=0, keepdims=True)
    grad_proj = grad_proj.astype(BF16)
    qkv_acc[...] += t_dot(normed, grad_proj)
    gn = dot_t(grad_proj, qkv_rel[...])
    context = ctx_ref[...]
    proj_acc[...] += t_dot(dot(context, head_spread[...]).astype(BF16), grad_out)
    out_part = (dot(context, proj_wide[...]) + mlp_part[0]).astype(BF16)
    mixed = (gn * vectors[0:1] + mlp_norm[0] * vectors[2:3]).astype(BF16)
    sums[0:1] += jnp.sum(gn * unit, axis=0, keepdims=True)
    sums[1:2] += jnp.sum(gn, axis=0, keepdims=True)

    @pl.when(step < 2)
    def _():
        partial_near[0, :, :D] = out_part
        partial_near[0, :, D:] = mixed

    @pl.when(step >= 2)
    def _():
        partial_far[0, :, :D] = out_part
        partial_far[0, :, D:] = mixed

    @pl.when(step == 0)
    def _():
        sums[2:3] = jnp.sum(grad_out.astype(F32), axis=0, keepdims=True)

    @pl.when(step == pl.num_programs(0) - 1)
    def _():
        width = 3 * QUART
        side = width + VEC_LANES
        vec = lax.broadcasted_iota(jnp.int32, (VEC_LANES, D), 0)
        out_bias = dot(sums[...].astype(BF16), to_rel[...])[2:3]
        small = dot(bias_sums[...].astype(BF16), place[...])
        rows = [sums[0:1], sums[1:2], mlp_sums[0:1], mlp_sums[1:2]]
        rows += [small[0:1, k * D : (k + 1) * D] for k in range(3)] + [out_bias]
        table = jnp.where(vec == 8 + rep[0], mlp_sums[2:3], 0.0)
        for index, line in enumerate(rows):
            table = jnp.where(vec == index, line, table)
        table = table.T.astype(BF16)
        keep[:, :width] = qkv_acc[:half].astype(BF16)
        send[:, :width] = qkv_acc[half:].astype(BF16)
        keep[:, width:side] = table[:half]
        send[:, width:side] = table[half:]
        for target, first in ((keep, 0), (send, QUART // 2)):
            piece = proj_acc[first : first + QUART // 2]
            block = min(block_rows, QUART // 2)
            for start in range(0, QUART // 2, block):
                for quarter in range(GROUP):
                    target[
                        start * GROUP + quarter * block : start * GROUP + (quarter + 1) * block, side:
                    ] = piece[start : start + block, quarter * QUART : (quarter + 1) * QUART].astype(BF16)


def whole(*shape):
    return pl.BlockSpec(shape, lambda i: (0,) * len(shape))


def token_block(count, width):
    return pl.BlockSpec((1, count, width), lambda i: (i, 0, 0))


PARAMS = pltpu.CompilerParams(vmem_limit_bytes=60 * 1024 * 1024)


def smem():
    return pl.BlockSpec(memory_space=pltpu.SMEM)


def run_mlp(packs, up_lo, up_hi, down_lo, down_hi, to_rel, rep, down_place):
    packed = packs[0].shape[0]
    own = (packed - 16) // 2
    half = D // 2
    wide = D + VEC_LANES
    grad = jax.ShapeDtypeStruct((half, 2 * D), BF16)
    acts = jax.ShapeDtypeStruct((GROUP, own, D), F32)
    return pl.pallas_call(
        functools.partial(mlp_kernel, down_place),
        grid=(GROUP,),
        in_specs=[whole(packed, D)] * 4
        + [whole(half, wide), whole(half, wide), whole(half, D), whole(half, D), whole(D, D), smem()],
        out_specs=[whole(half, 2 * D)] * 2 + [token_block(own, D)] * 3 + [whole(16, D), whole(8, D)],
        out_shape=[grad] * 2
        + [acts] * 2
        + [
            jax.ShapeDtypeStruct((GROUP, own, D), BF16),
            jax.ShapeDtypeStruct((16, D), F32), jax.ShapeDtypeStruct((8, D), F32)],
        scratch_shapes=[
            pltpu.VMEM((D, D), BF16),
            pltpu.VMEM((D, D), BF16),
            pltpu.VMEM((D, D), F32),
            pltpu.VMEM((D, D), F32),
        ],
        compiler_params=PARAMS,
        name="mlp",
    )(*packs, up_lo, up_hi, down_lo, down_hi, to_rel, rep)


def run_attention(packs, qkv_lo, qkv_hi, proj, to_rel, vectors, mlp_sums, place, head_spread, mlp_part, mlp_norm, values, rep, rows):
    packed = packs[0].shape[0]
    own = (packed - 16) // 2
    half = D // 2
    width = 3 * QUART
    column = np.arange(3 * EXT)
    which, head, unit = column // EXT, column % EXT // LANES, column % LANES
    inner = unit % HDIM
    halfway = ROT // 2
    partner = np.where(inner < halfway, inner + halfway, np.where(inner < ROT, inner - halfway, inner))
    source = which * QUART + head * HDIM + np.where(unit < HDIM, inner, partner)
    source = np.where((which == 2) & (unit >= HDIM), -1, source)
    spread = (jnp.arange(width)[:, None] == jnp.asarray(source, jnp.int32)[None, :]).astype(BF16)
    lane = np.arange(LANES) % HDIM
    angle = np.arange(LANES)[:, None] * (10000.0 ** (-(lane % halfway) / halfway))[None, :]
    sign = np.where(lane < halfway, -1.0, 1.0) * np.where(np.arange(LANES) < HDIM, 1.0, -1.0)
    turning = (lane < ROT)[None, :]
    tables = []
    for table in (np.where(turning, np.cos(angle), 1.0), np.where(turning, np.sin(angle) * sign, 0.0)):
        left = table.astype(np.float32)
        pieces = []
        for _ in range(3):
            piece = left.astype(BF16)
            pieces.append(piece)
            left = left - piece.astype(np.float32)
        tables.append(jnp.asarray(np.stack(pieces)))
    total = width + VEC_LANES + QUART
    grad = jax.ShapeDtypeStruct((half, total), BF16)
    part = jax.ShapeDtypeStruct((2, own, 2 * D), BF16)
    return pl.pallas_call(
        functools.partial(attention_kernel, rows),
        grid=(GROUP,),
        in_specs=[whole(packed, D)] * 4
        + [
            whole(half, width),
            whole(half, width),
            whole(QUART, D),
            whole(D, D),
            whole(16, D),
            whole(8, D),
            whole(width, 3 * D),
            whole(width, 3 * EXT),
            whole(EXT, QUART),
            whole(3, LANES, LANES),
            whole(3, LANES, LANES),
            token_block(own, D),
            token_block(own, D),
            token_block(own, D),
            smem(),
        ],
        out_specs=[
            whole(half, total),
            whole(half, total),
            pl.BlockSpec((1, own, 2 * D), lambda i: (jnp.minimum(i, 1), 0, 0)),
            pl.BlockSpec((1, own, 2 * D), lambda i: (jnp.maximum(i - 2, 0), 0, 0)),
        ],
        out_shape=[grad, grad, part, part],
        scratch_shapes=[
            pltpu.VMEM((D, 3 * EXT), BF16),
            pltpu.VMEM((EXT, D), BF16),
            pltpu.VMEM((8, 3 * EXT), F32),
            pltpu.VMEM((D, width), BF16),
            pltpu.VMEM((D, width), F32),
            pltpu.VMEM((QUART, D), F32),
            pltpu.VMEM((own, width), F32),
            pltpu.VMEM((own, EXT), BF16),
            pltpu.VMEM((8, D), F32),
            pltpu.VMEM((8, width), F32),
        ],
        compiler_params=PARAMS,
        name="attention",
    )(
        *packs, qkv_lo, qkv_hi, proj, to_rel, vectors, mlp_sums, place, spread, head_spread, *tables, mlp_part, mlp_norm,
        values, rep
    )


def finish_kernel(pack, near, received, to_rel, out_bias, live, block_out, input_grad):
    own = near.shape[0]
    partial = near[...].astype(F32) + received[...].astype(F32)
    block_out[...] = (live[...] * (pack[:own].astype(F32) + partial[:, :D] + out_bias[...])).astype(BF16)
    values = dot(pack[:own], to_rel[...])
    centered = values - jnp.mean(values, axis=-1, keepdims=True)
    inverse = lax.rsqrt(jnp.mean(centered * centered, axis=-1, keepdims=True) + EPSILON)
    unit = centered * inverse
    error = partial[:, D:]
    through = inverse * (
        error
        - jnp.mean(error, axis=-1, keepdims=True)
        - unit * jnp.mean(error * unit, axis=-1, keepdims=True)
    )
    grad = (dot(pack[own : 2 * own], to_rel[...]) + through).astype(BF16)
    input_grad[...] = dot_t(grad, to_rel[...]).astype(BF16)


def run_finish(pack, near, received, to_rel, out_bias, live):
    own = near.shape[0]
    out = jax.ShapeDtypeStruct((own, D), BF16)
    return pl.pallas_call(finish_kernel, out_shape=[out, out], compiler_params=PARAMS, name="finish")(
        pack, near, received, to_rel, out_bias, live
    )


def assemble_kernel(*refs):
    pairs, columns = refs[:4], refs[4:8]
    place = refs[8]
    qkv_out, proj_out, up_out, down_out, vec_out = refs[9:]
    rows = proj_out.shape[0]
    width = 3 * QUART
    side = width + VEC_LANES
    rep, top = place[0], place[1]

    def owner(values, natural):
        first, second, third, fourth = values
        chosen = jnp.where(rep == natural ^ 1, third, fourth)
        chosen = jnp.where(rep == natural ^ 2, second, chosen)
        return jnp.where(rep == natural, first, chosen)

    for natural in range(GROUP):
        down_out[natural * rows : (natural + 1) * rows] = owner([ref[:, :D].astype(F32) for ref in pairs], natural)
        up = owner([ref[:, D:].astype(F32) for ref in pairs], natural)
        for shard in range(D // rows):
            start = (shard * GROUP + natural) * rows
            up_out[:, start : start + rows] = up[:, shard * rows : (shard + 1) * rows]
        qkv = owner([ref[:, :width].astype(F32) for ref in columns], natural)
        for which in range(3):
            start = (which * GROUP + natural) * QUART
            qkv_out[:, start : start + QUART] = qkv[:, which * QUART : (which + 1) * QUART]
    parts = [ref[:, side:].astype(F32) for ref in columns]
    chosen = jnp.where((rep ^ top) == 1, parts[2], parts[3])
    chosen = jnp.where((rep ^ top) == 2, parts[1], chosen)
    proj_out[...] = jnp.where((rep ^ top) == 0, parts[0], chosen)
    vec = [ref[:, width:side].astype(F32) for ref in columns]
    vec_out[...] = ((vec[0] + vec[1]) + (vec[2] + vec[3])).T[:16]


def run_assemble(pairs, columns, place, rows):
    shapes = [(rows, 3 * D), (rows, D), (rows, FF), (GROUP * rows, D), (16, rows)]
    return pl.pallas_call(
        assemble_kernel,
        in_specs=[pl.BlockSpec(memory_space=pltpu.VMEM)] * 8 + [smem()],
        out_shape=[jax.ShapeDtypeStruct(shape, F32) for shape in shapes],
        compiler_params=PARAMS,
        name="assemble",
    )(*pairs, *columns, place)


def assemble_plain(pairs, columns, place, rows):
    width = 3 * QUART
    side = width + VEC_LANES
    rep, top = place[0], place[1]
    pairs = jnp.stack(pairs).astype(F32)
    columns = jnp.stack(columns).astype(F32)
    natural = jnp.arange(GROUP)
    swapped = natural ^ rep
    order = (swapped % 2) * 2 + swapped // 2
    pairs_nat, columns_nat = pairs[order], columns[order]
    qkv = columns_nat[:, :, :width].reshape(GROUP, rows, 3, QUART).transpose(1, 2, 0, 3)
    up = pairs_nat[:, :, D:].reshape(GROUP, rows, D // rows, rows).transpose(1, 2, 0, 3)
    vec = columns[:, :, width:side]
    vec = ((vec[0] + vec[1]) + (vec[2] + vec[3])).T[:16]
    return (
        qkv.reshape(rows, 3 * D),
        columns_nat[top][:, side:],
        up.reshape(rows, FF),
        pairs_nat[:, :, :D].reshape(GROUP * rows, D),
        vec,
    )


def quarter_kernel(*refs):
    vectors, (up, qkv, rep, up_own, qkv_own) = refs[:-5], refs[-5:]
    rows = up.shape[0]
    for natural in range(GROUP):

        @pl.when(rep[0] == natural)
        def _():
            for shard in range(D // rows):
                start = (shard * GROUP + natural) * rows
                up_own[:, shard * rows : (shard + 1) * rows] = up[:, start : start + rows]
            for which in range(3):
                start = (which * GROUP + natural) * QUART
                qkv_own[:, which * QUART : (which + 1) * QUART] = qkv[:, start : start + QUART]

    lines = [ref[k : k + 1].astype(F32) for ref in vectors for k in range(ref.shape[0])]
    index = lax.broadcasted_iota(jnp.int32, (VEC_LANES, rows), 0)
    table = jnp.zeros((VEC_LANES, rows), F32)
    for place, line in enumerate(lines):
        table = jnp.where(index == place, line, table)
    up_own[:, D:] = table.T.astype(BF16)


def run_quarter(up, qkv, vectors, rep):
    rows = up.shape[0]
    return pl.pallas_call(
        quarter_kernel,
        in_specs=[pl.BlockSpec(memory_space=pltpu.VMEM)] * (2 + len(vectors)) + [smem()],
        out_shape=[
            jax.ShapeDtypeStruct((rows, D + VEC_LANES), BF16),
            jax.ShapeDtypeStruct((rows, 3 * QUART), BF16),
        ],
        compiler_params=PARAMS,
        name="quarter",
    )(*vectors, up, qkv, rep)


def make_body(shards):
    bits = shards.bit_length() - 1
    rows = D // shards
    lowest_first = [1 << k for k in range(bits)]
    highest_first = lowest_first[::-1]

    def reverse(value, width):
        return sum(((value >> k) & 1) << (width - 1 - k) for k in range(width))

    def shard_swap(value, mask):
        return lax.ppermute(value, "fsdp", [(i, i ^ mask) for i in range(shards)])

    def core_swap(value):
        return lax.ppermute(value, "rep", [(i, i ^ 1) for i in range(GROUP)])

    def x_swap(value):
        return lax.ppermute(value, "rep", [(i, i ^ 2) for i in range(GROUP)])

    down_order = highest_first if rows % 16 else lowest_first[:1] + highest_first[:-1]
    down_place = [
        reverse(sum(mask for k, mask in enumerate(down_order) if (p >> k) & 1), bits) for p in range(shards)
    ]

    def gather_all(own, order=highest_first):
        for mask in order[:-1]:
            own = jnp.concatenate([own, shard_swap(own, mask)], axis=0)
        return own, shard_swap(own, order[-1])

    def add(keep, received):
        return keep.astype(F32) + received.astype(F32)

    def reduce_all(keep, send):
        for mask in lowest_first:
            total = add(keep, shard_swap(send, mask)).astype(BF16)
            half = total.shape[0] // 2
            keep, send = total[:half], total[half:]
        return total

    def one_hot(count, width, mine):
        place = jnp.array([reverse(p, width) for p in range(count)], jnp.int32)
        natural = ((place ^ mine)[:, None] * rows + jnp.arange(rows)[None, :]).reshape(1, count * rows)
        return (jnp.arange(count * rows)[:, None] == natural).astype(BF16)

    def body(
        block_input,
        segment_ids,
        out_cotangent,
        first_gain,
        first_shift,
        second_gain,
        second_shift,
        qkv_weight,
        qkv_bias,
        proj_weight,
        proj_bias,
        up_weight,
        up_bias,
        down_weight,
        down_bias,
    ):
        micro, slot = block_input.shape[0], block_input.shape[1]
        own_tokens = micro * slot
        mine = lax.axis_index("fsdp")
        rep = lax.axis_index("rep")
        core = rep % 2
        across = rep // 2
        top = mine // (shards // 4)
        top_across, top_core = top // 2, top % 2

        rep_ref = rep.reshape(1)
        vectors_own = [
            value.reshape(-1, rows)
            for value in (
                first_gain, first_shift, second_gain, second_shift, qkv_bias, proj_bias, up_bias, down_bias
            )
        ]
        if rows % 32:
            vector_own = jnp.pad(jnp.concatenate(vectors_own, axis=0), ((0, VEC_LANES - 13), (0, 0))).T
            up_own = lax.dynamic_index_in_dim(
                up_weight.reshape(rows, shards, GROUP, rows), rep, axis=2, keepdims=False
            ).reshape(rows, D)
            up_own = jnp.concatenate([up_own, vector_own], axis=1)
            qkv_own = lax.dynamic_index_in_dim(
                qkv_weight.reshape(rows, 3, GROUP, QUART), rep, axis=2, keepdims=False
            ).reshape(rows, 3 * QUART)
        else:
            up_own, qkv_own = run_quarter(up_weight, qkv_weight, vectors_own, rep_ref)
        down_own = lax.dynamic_index_in_dim(
            down_weight.reshape(GROUP, rows, D), rep, axis=0, keepdims=False
        )

        live = (segment_ids.reshape(own_tokens, 1) >= 0).astype(F32)
        own_input = block_input.reshape(own_tokens, D)
        own_grad = (out_cotangent.reshape(own_tokens, D).astype(F32) * live).astype(BF16)
        segment_row = jnp.pad(
            segment_ids.reshape(1, own_tokens).astype(BF16), ((0, 15), (0, D - own_tokens))
        )
        token_pack = jnp.concatenate([own_input, own_grad, segment_row], axis=0)
        token_across = x_swap(token_pack)
        token_beside = core_swap(token_pack)
        token_far = core_swap(token_across)
        packs = (token_pack, token_across, token_beside, token_far)

        up_lo, up_hi = gather_all(up_own)
        down_lo, down_hi = gather_all(down_own, down_order)
        qkv_lo, qkv_hi = gather_all(qkv_own)

        proj_part = jnp.where(top_across == across, proj_weight, shard_swap(proj_weight, highest_first[0]))
        proj_part = jnp.where(top_core == core, proj_part, shard_swap(proj_part, highest_first[1]))
        for mask in highest_first[2:]:
            proj_part = jnp.concatenate([proj_part, shard_swap(proj_part, mask)], axis=0)

        to_rel = one_hot(shards, bits, mine)
        head_to_rel = one_hot(shards // 4, bits - 2, mine % (shards // 4))
        head_spread = jnp.pad(
            head_to_rel.reshape(LOCAL_HEADS, HDIM, QUART), ((0, 0), (0, LANES - HDIM), (0, 0))
        ).reshape(EXT, QUART)

        width = 3 * QUART
        place = jnp.array([reverse(p, bits) for p in range(shards)], jnp.int32)
        shard_start = (place ^ mine)[None, :, None] * (3 * rows)
        found = shard_start + jnp.arange(3)[:, None, None] * rows + jnp.arange(rows)[None, None, :]
        found = found.reshape(1, 3 * D)
        found = jnp.where(found % D // QUART == rep, found // D * QUART + found % QUART, -1)
        bias_place = (jnp.arange(width)[:, None] == found).astype(BF16)

        keep, send, mlp_part, mlp_norm, values, vectors, mlp_sums = run_mlp(
            packs, up_lo, up_hi, down_lo, down_hi, to_rel, rep_ref, down_place
        )
        pair = reduce_all(keep, send)
        keep, send, partial, partial_far = run_attention(
            packs, qkv_lo, qkv_hi, proj_part, to_rel, vectors, mlp_sums, bias_place, head_spread,
            mlp_part, mlp_norm, values, rep_ref, rows,
        )

        side = width + VEC_LANES
        for mask in lowest_first[:-2]:
            total = add(keep, shard_swap(send, mask)).astype(BF16)
            half = total.shape[0] // 2
            keep, send = total[:half], total[half:]
        columns, proj_block = total[:, :side], total[:, side:]
        proj_block = jnp.concatenate([proj_block[: 2 * rows], proj_block[2 * rows :]], axis=1)
        packed = jnp.concatenate([columns[2 * rows :], proj_block], axis=1)
        sent = shard_swap(packed, lowest_first[-2])
        columns = add(columns[: 2 * rows], sent[:, :side])
        proj_block = add(proj_block, sent[:, side:])
        proj_block = jnp.concatenate(
            [
                proj_block[:rows, :QUART],
                proj_block[rows:, :QUART],
                proj_block[:rows, QUART:],
                proj_block[rows:, QUART:],
            ],
            axis=1,
        ).astype(BF16)
        packed = jnp.concatenate([columns[rows:].astype(BF16), proj_block], axis=1)
        own = jnp.concatenate([columns[:rows].astype(BF16), proj_block], axis=1)
        column = add(own, shard_swap(packed, lowest_first[-1])).astype(BF16)

        summed = add(partial, core_swap(partial_far))
        received = x_swap(summed[1].astype(BF16))
        vectors_nat = dot_t(vectors.astype(BF16), to_rel)
        out_bias = (vectors_nat[7] + vectors_nat[12])[None]
        block_out, input_grad = run_finish(token_pack, summed[0], received, to_rel, out_bias, live)

        pair_across = x_swap(pair)
        pair_all = (pair, pair_across, core_swap(pair), core_swap(pair_across))
        column_across = x_swap(column)
        column_all = (column, column_across, core_swap(column), core_swap(column_across))
        assemble = assemble_plain if rows % 32 else run_assemble
        qkv_out, proj_out, up_out, down_out, vec_out = assemble(
            pair_all, column_all, jnp.stack([rep, top]), rows
        )
        return (
            block_out.reshape(micro, slot, D),
            input_grad.reshape(micro, slot, D),
            vec_out[0],
            vec_out[1],
            vec_out[2],
            vec_out[3],
            qkv_out,
            vec_out[4:7].reshape(3 * rows),
            proj_out,
            vec_out[7],
            up_out,
            vec_out[8:12].reshape(GROUP * rows),
            down_out,
            vec_out[7],
        )

    return body


def solution(mesh):
    in_specs = (
        P(None, ("fsdp", "rep"), None),
        P(None, ("fsdp", "rep")),
        P(None, ("fsdp", "rep"), None),
        P("fsdp"),
        P("fsdp"),
        P("fsdp"),
        P("fsdp"),
        P("fsdp", None),
        P("fsdp"),
        P("fsdp", None),
        P("fsdp"),
        P("fsdp", None),
        P("fsdp"),
        P("fsdp", None),
        P("fsdp"),
    )
    out_specs = (
        P(None, ("fsdp", "rep"), None),
        P(None, ("fsdp", "rep"), None),
        P("fsdp"),
        P("fsdp"),
        P("fsdp"),
        P("fsdp"),
        P("fsdp", None),
        P("fsdp"),
        P("fsdp", None),
        P("fsdp"),
        P("fsdp", None),
        P("fsdp"),
        P("fsdp", None),
        P("fsdp"),
    )
    plain = make_body(mesh.shape["fsdp"])

    return jax.shard_map(plain, mesh=mesh, in_specs=in_specs, out_specs=out_specs, check_vma=False)
```

```python
import functools

import jax
import jax.numpy as jnp
import numpy as np
from jax import lax
from jax.experimental import pallas as pl
from jax.experimental.pallas import tpu as pltpu
from jax.sharding import PartitionSpec as P


D = 768
HEADS = 12
HDIM = 64
ROT = 16
FF = 3072
GROUP = 4
QUART = D // GROUP
LOCAL_HEADS = HEADS // GROUP
VEC_LANES = 128

EPSILON = 1e-05
NEG_FILL = -1e30
BF16 = jnp.bfloat16
F32 = jnp.float32


def dot(left, right):
    return jnp.dot(left, right, preferred_element_type=F32)


def dot_t(left, right):
    return lax.dot_general(left, right, (((1,), (1,)), ((), ())), preferred_element_type=F32)


def t_dot(left, right):
    return lax.dot_general(left, right, (((0,), (0,)), ((), ())), preferred_element_type=F32)


LANES = 128
EXT = LOCAL_HEADS * LANES


def layer_norm(values, gain_a, shift_a):
    centered = values - jnp.mean(values, axis=-1, keepdims=True)
    variance = jnp.mean(centered * centered, axis=-1, keepdims=True)
    inverse = lax.rsqrt(variance + EPSILON)
    unit = centered * inverse
    return (unit * gain_a + shift_a).astype(BF16), unit


def take(step, refs, rows):
    value = refs[-1][rows]
    for place in range(len(refs) - 2, -1, -1):
        value = jnp.where(step == place, refs[place][rows], value)
    return value


def hot(rows, columns):
    return jnp.where(rows == columns, 1.0, 0.0).astype(BF16)


def mlp_forward_kernel(
    down_place,
    near, across, beside, far, up_lo, up_hi, natural, rep,
    keep, send, slope_out, act_out, unit_out, grad_out_ref, vectors_out, up_rel, to_rel,
    down_acc,
):
    step = pl.program_id(0)
    packs = (near, across, beside, far)
    own = (near.shape[0] - 16) // 2
    half = D // 2

    @pl.when(step == 0)
    def _():
        to_rel[...] = hot(lax.broadcasted_iota(jnp.int32, (D, D), 0), natural[...])
        up_rel[:half] = dot(up_lo[:, :D], to_rel[...]).astype(BF16)
        up_rel[half:] = dot(up_hi[:, :D], to_rel[...]).astype(BF16)
        vectors_out[:, :half] = up_lo[:, D:].astype(F32).T[:16]
        vectors_out[:, half:] = up_hi[:, D:].astype(F32).T[:16]
        down_acc[...] = jnp.zeros_like(down_acc)

    inputs = take(step, packs, slice(0, own))
    rest = take(step, packs, slice(own, 2 * own + 16))
    grad_out_ref[0] = rest
    grad_out = rest[:own]
    normed, unit = layer_norm(dot(inputs, to_rel[...]), vectors_out[2:3], vectors_out[3:4])
    unit_out[0] = unit
    bias = vectors_out[11:12]
    for quarter in range(GROUP - 1):
        bias = jnp.where(rep[0] == quarter, vectors_out[8 + quarter : 9 + quarter], bias)
    pre_act = dot(normed, up_rel[...]) + bias
    phi = 0.5 * (1.0 + lax.erf(pre_act * 0.7071067811865476))
    activ = (pre_act * phi).astype(BF16)
    slope_out[0] = phi + pre_act * jnp.exp(-0.5 * pre_act * pre_act) * 0.3989422804014327
    act_out[0] = activ
    down_acc[...] += t_dot(activ, grad_out)

    @pl.when(step == pl.num_programs(0) - 1)
    def _():
        if down_place == sorted(down_place):
            keep[...] = down_acc[:half].astype(BF16)
            send[...] = down_acc[half:].astype(BF16)
        else:
            block = D // len(down_place)
            for target, source in enumerate(down_place):
                piece = send if target * block >= half else keep
                start = target * block % half
                piece[start : start + block] = down_acc[source * block : (source + 1) * block].astype(BF16)


def mlp_backward_kernel(
    cotangents, down_lo, down_hi, up_rel, to_rel, slope, act, unit_ref, vectors,
    keep, send, out_part, grad_norm, sums,
    down_rel, up_acc,
):
    step = pl.program_id(0)
    half = D // 2

    @pl.when(step == 0)
    def _():
        down_rel[:half] = down_lo[...]
        down_rel[half:] = down_hi[...]
        up_acc[...] = jnp.zeros_like(up_acc)
        sums[...] = jnp.zeros_like(sums)

    unit = unit_ref[0]
    grad_out = cotangents[0, : unit.shape[0]]
    normed = (unit * vectors[2:3] + vectors[3:4]).astype(BF16)
    grad_pre = dot_t(grad_out, down_rel[...]) * slope[0]
    grad_pre_b = grad_pre.astype(BF16)
    up_acc[...] += t_dot(normed, grad_pre_b)
    gn = dot_t(grad_pre_b, up_rel[...])
    out_part[0] = dot(act[0], down_rel[...])
    grad_norm[0] = gn
    sums[0:1] += jnp.sum(gn * unit, axis=0, keepdims=True)
    sums[1:2] += jnp.sum(gn, axis=0, keepdims=True)
    sums[2:3] += jnp.sum(grad_pre, axis=0, keepdims=True)

    @pl.when(step == pl.num_programs(0) - 1)
    def _():
        keep[...] = dot_t(up_acc[:half].astype(BF16), to_rel[...]).astype(BF16)
        send[...] = dot_t(up_acc[half:].astype(BF16), to_rel[...]).astype(BF16)


def attention_kernel(
    block_rows,
    cotangents, qkv_lo, qkv_hi, proj, to_rel, vectors, mlp_sums, found, source, head_natural,
    cosines, sines, mlp_part, mlp_norm, values, rep,
    keep, send, partial_near, partial_far,
    wide, proj_wide, bias_wide, qkv_rel, qkv_acc, proj_acc, gp_ref, ctx_ref, sums, bias_sums, place, spread, head_spread,
):
    step = pl.program_id(0)
    half = D // 2
    own = cotangents.shape[1] - 16

    @pl.when(step == 0)
    def _():
        width = 3 * QUART
        place[...] = hot(lax.broadcasted_iota(jnp.int32, (width, 3 * D), 0), found[...])
        spread[...] = hot(lax.broadcasted_iota(jnp.int32, (width, 3 * EXT), 0), source[...])
        padded = lax.broadcasted_iota(jnp.int32, (EXT, QUART), 0)
        padded = jnp.where(padded % LANES < HDIM, padded // LANES * HDIM + padded % LANES, -1)
        head_spread[...] = hot(padded, head_natural[...])
        qkv_rel[:half] = qkv_lo[...]
        qkv_rel[half:] = qkv_hi[...]
        wide[:half] = dot(qkv_lo[...], spread[...]).astype(BF16)
        wide[half:] = dot(qkv_hi[...], spread[...]).astype(BF16)
        proj_wide[...] = dot(head_spread[...], proj[...]).astype(BF16)
        vectors_b = vectors[...].astype(BF16)
        bias = sum(dot_t(vectors_b[4 + k : 5 + k], place[:, k * D : (k + 1) * D]) for k in range(3))
        bias = jnp.broadcast_to(bias, (8, bias.shape[1])).astype(BF16)
        bias_wide[...] = dot(bias, spread[...])
        qkv_acc[...] = jnp.zeros_like(qkv_acc)
        proj_acc[...] = jnp.zeros_like(proj_acc)
        sums[...] = jnp.zeros_like(sums)
        bias_sums[...] = jnp.zeros_like(bias_sums)

    grad_out = cotangents[0, :own]
    segment_row = cotangents[0, own:].astype(F32)
    unit = values[0]
    normed = (unit * vectors[0:1] + vectors[1:2]).astype(BF16)
    projected = dot(normed, wide[...]) + bias_wide[0:1]
    grad_context = dot_t(grad_out, proj_wide[...]).astype(BF16)
    lane = lax.broadcasted_iota(jnp.int32, (LANES, LANES), 1)
    sublane = lax.broadcasted_iota(jnp.int32, (LANES, LANES), 0)
    lower = lane < HDIM
    units = [(slab, head) for slab in range(own // LANES) for head in range(LOCAL_HEADS)]
    allowed, cos, sin = [], [], []
    for slab in range(own // LANES):
        seg_keys = jnp.broadcast_to(segment_row[0:1, slab * LANES : (slab + 1) * LANES], (LANES, LANES))
        same = seg_keys == seg_keys.T
        allowed.append(same & (lane <= sublane))
        position = jnp.sum(jnp.where(same & (lane < sublane), 1.0, 0.0), axis=1, keepdims=True)
        pick = (lane.astype(F32) == position).astype(BF16)
        cos.append(dot(pick, cosines[0]) + dot(pick, cosines[1]) + dot(pick, cosines[2]))
        sin.append(dot(pick, sines[0]) + dot(pick, sines[1]) + dot(pick, sines[2]))

    def part(value, unit, which):
        slab, head = unit
        start = which * EXT + head * LANES
        return value[slab * LANES : (slab + 1) * LANES, start : start + LANES]

    def turn(value, slab, direction):
        return value * cos[slab] + direction * (pltpu.roll(value, HDIM, 1) * sin[slab])

    query = [(turn(part(projected, u, 0), u[0], 1.0) * 0.125).astype(BF16) for u in units]
    key = [turn(part(projected, u, 1), u[0], 1.0).astype(BF16) for u in units]
    value = [part(projected, u, 2).astype(BF16) for u in units]
    gctx = [part(grad_context, u, 0) for u in units]
    count = range(len(units))
    scores = [dot_t(jnp.where(lower, query[n], jnp.zeros_like(query[n])), key[n]) for n in count]
    grad_probs = [dot_t(gctx[n], value[n]) for n in count]
    scores = [jnp.where(allowed[units[n][0]], scores[n], NEG_FILL) for n in count]
    weight = [jnp.exp(score - jnp.max(score, axis=-1, keepdims=True)) for score in scores]
    probs = [each * (1.0 / jnp.sum(each, axis=-1, keepdims=True)) for each in weight]
    probs_b = [each.astype(BF16) for each in probs]
    context = [dot(probs_b[n], value[n]) for n in count]
    grad_value = [t_dot(probs_b[n], gctx[n]) for n in count]
    delta = [jnp.sum(probs[n] * grad_probs[n], axis=-1, keepdims=True) for n in count]
    grad_sc = [(probs[n] * (grad_probs[n] - delta[n])).astype(BF16) for n in count]
    grad_query = [dot(grad_sc[n], key[n]) for n in count]
    grad_key = [t_dot(grad_sc[n], query[n]) for n in count]
    for n, (slab, head) in enumerate(units):
        row = slice(slab * LANES, (slab + 1) * LANES)
        ctx_ref[row, head * LANES : (head + 1) * LANES] = context[n].astype(BF16)
        turned = (
            turn(grad_query[n] * 0.125, slab, -1.0),
            turn(grad_key[n], slab, -1.0),
            grad_value[n],
        )
        for which, grad in enumerate(turned):
            start = which * QUART + head * HDIM
            gp_ref[row, start : start + HDIM] = grad[:, :HDIM]

    grad_proj = gp_ref[...]
    bias_sums[0:1] += jnp.sum(grad_proj, axis=0, keepdims=True)
    grad_proj = grad_proj.astype(BF16)
    qkv_acc[...] += t_dot(normed, grad_proj)
    gn = dot_t(grad_proj, qkv_rel[...])
    context = ctx_ref[...]
    proj_acc[...] += t_dot(dot(context, head_spread[...]).astype(BF16), grad_out)
    out_part = (dot(context, proj_wide[...]) + mlp_part[0]).astype(BF16)
    mixed = (gn * vectors[0:1] + mlp_norm[0] * vectors[2:3]).astype(BF16)
    sums[0:1] += jnp.sum(gn * unit, axis=0, keepdims=True)
    sums[1:2] += jnp.sum(gn, axis=0, keepdims=True)

    @pl.when(step < 2)
    def _():
        partial_near[0, :, :D] = out_part
        partial_near[0, :, D:] = mixed

    @pl.when(step >= 2)
    def _():
        partial_far[0, :, :D] = out_part
        partial_far[0, :, D:] = mixed

    @pl.when(step == 0)
    def _():
        sums[2:3] = jnp.sum(grad_out.astype(F32), axis=0, keepdims=True)

    @pl.when(step == pl.num_programs(0) - 1)
    def _():
        width = 3 * QUART
        side = width + VEC_LANES
        vec = lax.broadcasted_iota(jnp.int32, (VEC_LANES, D), 0)
        out_bias = dot(sums[...].astype(BF16), to_rel[...])[2:3]
        small = dot(bias_sums[...].astype(BF16), place[...])
        rows = [sums[0:1], sums[1:2], mlp_sums[0:1], mlp_sums[1:2]]
        rows += [small[0:1, k * D : (k + 1) * D] for k in range(3)] + [out_bias]
        table = jnp.where(vec == 8 + rep[0], mlp_sums[2:3], 0.0)
        for index, line in enumerate(rows):
            table = jnp.where(vec == index, line, table)
        table = table.T.astype(BF16)
        keep[:, :width] = qkv_acc[:half].astype(BF16)
        send[:, :width] = qkv_acc[half:].astype(BF16)
        keep[:, width:side] = table[:half]
        send[:, width:side] = table[half:]
        for target, first in ((keep, 0), (send, QUART // 2)):
            piece = proj_acc[first : first + QUART // 2]
            block = min(block_rows, QUART // 2)
            for start in range(0, QUART // 2, block):
                for quarter in range(GROUP):
                    target[
                        start * GROUP + quarter * block : start * GROUP + (quarter + 1) * block, side:
                    ] = piece[start : start + block, quarter * QUART : (quarter + 1) * QUART].astype(BF16)


def whole(*shape):
    return pl.BlockSpec(shape, lambda i: (0,) * len(shape))


def token_block(count, width):
    return pl.BlockSpec((1, count, width), lambda i: (i, 0, 0))


PARAMS = pltpu.CompilerParams(vmem_limit_bytes=60 * 1024 * 1024)


def smem():
    return pl.BlockSpec(memory_space=pltpu.SMEM)


def run_mlp_forward(packs, up_lo, up_hi, natural, rep, down_place):
    packed = packs[0].shape[0]
    own = (packed - 16) // 2
    half = D // 2
    wide = D + VEC_LANES
    grad = jax.ShapeDtypeStruct((half, D), BF16)
    return pl.pallas_call(
        functools.partial(mlp_forward_kernel, down_place),
        grid=(GROUP,),
        in_specs=[whole(packed, D)] * 4 + [whole(half, wide), whole(half, wide), whole(1, D), smem()],
        out_specs=[whole(half, D)] * 2
        + [token_block(own, D)] * 3
        + [token_block(own + 16, D), whole(16, D), whole(D, D), whole(D, D)],
        out_shape=[
            grad,
            grad,
            jax.ShapeDtypeStruct((GROUP, own, D), F32),
            jax.ShapeDtypeStruct((GROUP, own, D), BF16),
            jax.ShapeDtypeStruct((GROUP, own, D), F32),
            jax.ShapeDtypeStruct((GROUP, own + 16, D), BF16),
            jax.ShapeDtypeStruct((16, D), F32),
            jax.ShapeDtypeStruct((D, D), BF16),
            jax.ShapeDtypeStruct((D, D), BF16),
        ],
        scratch_shapes=[pltpu.VMEM((D, D), F32)],
        compiler_params=PARAMS,
        name="mlp_forward",
    )(*packs, up_lo, up_hi, natural, rep)


def run_mlp_backward(cotangents, down_lo, down_hi, up_rel, to_rel, pre, act, values, vectors):
    own = cotangents.shape[1] - 16
    half = D // 2
    grad = jax.ShapeDtypeStruct((half, D), BF16)
    acts = jax.ShapeDtypeStruct((GROUP, own, D), F32)
    return pl.pallas_call(
        mlp_backward_kernel,
        grid=(GROUP,),
        in_specs=[token_block(own + 16, D), whole(half, D), whole(half, D), whole(D, D), whole(D, D)]
        + [token_block(own, D)] * 3
        + [whole(16, D)],
        out_specs=[whole(half, D)] * 2 + [token_block(own, D)] * 2 + [whole(8, D)],
        out_shape=[grad, grad, acts, acts, jax.ShapeDtypeStruct((8, D), F32)],
        scratch_shapes=[pltpu.VMEM((D, D), BF16), pltpu.VMEM((D, D), F32)],
        compiler_params=PARAMS,
        name="mlp_backward",
    )(cotangents, down_lo, down_hi, up_rel, to_rel, pre, act, values, vectors)


def run_attention(cotangents, qkv_lo, qkv_hi, proj, to_rel, vectors, mlp_sums, found, head_natural, mlp_part, mlp_norm, values, rep, rows):
    own = cotangents.shape[1] - 16
    half = D // 2
    width = 3 * QUART
    column = np.arange(3 * EXT)
    which, head, unit = column // EXT, column % EXT // LANES, column % LANES
    inner = unit % HDIM
    halfway = ROT // 2
    partner = np.where(inner < halfway, inner + halfway, np.where(inner < ROT, inner - halfway, inner))
    source = which * QUART + head * HDIM + np.where(unit < HDIM, inner, partner)
    source = np.where((which == 2) & (unit >= HDIM), -1, source)
    source = jnp.asarray(source[None, :], jnp.int32)
    lane = np.arange(LANES) % HDIM
    angle = np.arange(LANES)[:, None] * (10000.0 ** (-(lane % halfway) / halfway))[None, :]
    sign = np.where(lane < halfway, -1.0, 1.0) * np.where(np.arange(LANES) < HDIM, 1.0, -1.0)
    turning = (lane < ROT)[None, :]
    tables = []
    for table in (np.where(turning, np.cos(angle), 1.0), np.where(turning, np.sin(angle) * sign, 0.0)):
        left = table.astype(np.float32)
        pieces = []
        for _ in range(3):
            piece = left.astype(BF16)
            pieces.append(piece)
            left = left - piece.astype(np.float32)
        tables.append(jnp.asarray(np.stack(pieces)))
    total = width + VEC_LANES + QUART
    grad = jax.ShapeDtypeStruct((half, total), BF16)
    part = jax.ShapeDtypeStruct((2, own, 2 * D), BF16)
    return pl.pallas_call(
        functools.partial(attention_kernel, rows),
        grid=(GROUP,),
        in_specs=[
            token_block(own + 16, D),
            whole(half, width),
            whole(half, width),
            whole(QUART, D),
            whole(D, D),
            whole(16, D),
            whole(8, D),
            whole(1, 3 * D),
            whole(1, 3 * EXT),
            whole(1, QUART),
            whole(3, LANES, LANES),
            whole(3, LANES, LANES),
            token_block(own, D),
            token_block(own, D),
            token_block(own, D),
            smem(),
        ],
        out_specs=[
            whole(half, total),
            whole(half, total),
            pl.BlockSpec((1, own, 2 * D), lambda i: (jnp.minimum(i, 1), 0, 0)),
            pl.BlockSpec((1, own, 2 * D), lambda i: (jnp.maximum(i - 2, 0), 0, 0)),
        ],
        out_shape=[grad, grad, part, part],
        scratch_shapes=[
            pltpu.VMEM((D, 3 * EXT), BF16),
            pltpu.VMEM((EXT, D), BF16),
            pltpu.VMEM((8, 3 * EXT), F32),
            pltpu.VMEM((D, width), BF16),
            pltpu.VMEM((D, width), F32),
            pltpu.VMEM((QUART, D), F32),
            pltpu.VMEM((own, width), F32),
            pltpu.VMEM((own, EXT), BF16),
            pltpu.VMEM((8, D), F32),
            pltpu.VMEM((8, width), F32),
            pltpu.VMEM((width, 3 * D), BF16),
            pltpu.VMEM((width, 3 * EXT), BF16),
            pltpu.VMEM((EXT, QUART), BF16),
        ],
        compiler_params=PARAMS,
        name="attention",
    )(
        cotangents, qkv_lo, qkv_hi, proj, to_rel, vectors, mlp_sums, found, source, head_natural, *tables, mlp_part, mlp_norm,
        values, rep
    )


def finish_kernel(pack, near, received, to_rel, vectors, live, block_out, input_grad):
    vectors_nat = dot_t(vectors[...].astype(BF16), to_rel[...])
    out_bias = vectors_nat[7:8] + vectors_nat[12:13]
    own = near.shape[0]
    partial = near[...].astype(F32) + received[...].astype(F32)
    block_out[...] = (live[...] * (pack[:own].astype(F32) + partial[:, :D] + out_bias)).astype(BF16)
    values = dot(pack[:own], to_rel[...])
    centered = values - jnp.mean(values, axis=-1, keepdims=True)
    inverse = lax.rsqrt(jnp.mean(centered * centered, axis=-1, keepdims=True) + EPSILON)
    unit = centered * inverse
    error = partial[:, D:]
    through = inverse * (
        error
        - jnp.mean(error, axis=-1, keepdims=True)
        - unit * jnp.mean(error * unit, axis=-1, keepdims=True)
    )
    grad = (dot(pack[own : 2 * own], to_rel[...]) + through).astype(BF16)
    input_grad[...] = dot_t(grad, to_rel[...]).astype(BF16)


def run_finish(pack, near, received, to_rel, vectors, live):
    own = near.shape[0]
    out = jax.ShapeDtypeStruct((own, D), BF16)
    return pl.pallas_call(finish_kernel, out_shape=[out, out], compiler_params=PARAMS, name="finish")(
        pack, near, received, to_rel, vectors, live
    )


def owner(values, rep, natural):
    first, second, third, fourth = values
    chosen = jnp.where(rep == natural ^ 1, third, fourth)
    chosen = jnp.where(rep == natural ^ 2, second, chosen)
    return jnp.where(rep == natural, first, chosen)


def assemble_mlp_kernel(*refs):
    pairs, rep, up_out, down_out = refs[:4], refs[4][0], refs[5], refs[6]
    rows = up_out.shape[0]
    for natural in range(GROUP):
        down_out[natural * rows : (natural + 1) * rows] = owner([ref[:, :D].astype(F32) for ref in pairs], rep, natural)
        up = owner([ref[:, D:].astype(F32) for ref in pairs], rep, natural)
        for shard in range(D // rows):
            start = (shard * GROUP + natural) * rows
            up_out[:, start : start + rows] = up[:, shard * rows : (shard + 1) * rows]


def run_assemble_mlp(pairs, place, rows):
    return pl.pallas_call(
        assemble_mlp_kernel,
        in_specs=[pl.BlockSpec(memory_space=pltpu.VMEM)] * 4 + [smem()],
        out_shape=[jax.ShapeDtypeStruct((rows, FF), F32), jax.ShapeDtypeStruct((GROUP * rows, D), F32)],
        compiler_params=PARAMS,
        name="assemble_mlp",
    )(*pairs, place)


def assemble_mlp_plain(pairs, place, rows):
    swapped = jnp.arange(GROUP) ^ place[0]
    pairs_nat = jnp.stack(pairs).astype(F32)[(swapped % 2) * 2 + swapped // 2]
    up = pairs_nat[:, :, D:].reshape(GROUP, rows, D // rows, rows).transpose(1, 2, 0, 3)
    return up.reshape(rows, FF), pairs_nat[:, :, :D].reshape(GROUP * rows, D)


VEC_PARTS = (1, 1, 1, 1, 3, 1, GROUP)


def assemble_kernel(*refs):
    columns, place = refs[:4], refs[4]
    qkv_out, proj_out, vec_outs = refs[5], refs[6], refs[7:]
    rows = proj_out.shape[0]
    width = 3 * QUART
    side = width + VEC_LANES
    rep, top = place[0], place[1]
    for natural in range(GROUP):
        qkv = owner([ref[:, :width].astype(F32) for ref in columns], rep, natural)
        for which in range(3):
            start = (which * GROUP + natural) * QUART
            qkv_out[:, start : start + QUART] = qkv[:, which * QUART : (which + 1) * QUART]
    proj_out[...] = owner([ref[:, side:].astype(F32) for ref in columns], rep, top)
    vec = [ref[:, width:side].astype(F32) for ref in columns]
    vec = ((vec[0] + vec[1]) + (vec[2] + vec[3])).T[:16]
    line = 0
    for out in vec_outs:
        for start in range(0, out.shape[1], rows):
            out[:, start : start + rows] = vec[line : line + 1]
            line += 1


def run_assemble(columns, place, rows):
    shapes = [(rows, 3 * D), (rows, D)] + [(1, count * rows) for count in VEC_PARTS]
    return pl.pallas_call(
        assemble_kernel,
        in_specs=[pl.BlockSpec(memory_space=pltpu.VMEM)] * 4 + [smem()],
        out_shape=[jax.ShapeDtypeStruct(shape, F32) for shape in shapes],
        compiler_params=PARAMS,
        name="assemble",
    )(*columns, place)


def assemble_plain(columns, place, rows):
    width = 3 * QUART
    side = width + VEC_LANES
    columns = jnp.stack(columns).astype(F32)
    swapped = jnp.arange(GROUP) ^ place[0]
    columns_nat = columns[(swapped % 2) * 2 + swapped // 2]
    qkv = columns_nat[:, :, :width].reshape(GROUP, rows, 3, QUART).transpose(1, 2, 0, 3)
    vec = columns[:, :, width:side]
    vec = ((vec[0] + vec[1]) + (vec[2] + vec[3])).T
    outs, line = [], 0
    for count in VEC_PARTS:
        outs.append(vec[line : line + count].reshape(1, count * rows))
        line += count
    return (qkv.reshape(rows, 3 * D), columns_nat[place[1]][:, side:], *outs)


def quarter_kernel(*refs):
    vectors, (up, qkv, rep, up_own, qkv_own) = refs[:-5], refs[-5:]
    rows = up.shape[0]
    for natural in range(GROUP):

        @pl.when(rep[0] == natural)
        def _():
            for shard in range(D // rows):
                start = (shard * GROUP + natural) * rows
                up_own[:, shard * rows : (shard + 1) * rows] = up[:, start : start + rows]
            for which in range(3):
                start = (which * GROUP + natural) * QUART
                qkv_own[:, which * QUART : (which + 1) * QUART] = qkv[:, start : start + QUART]

    lines = [
        ref[:, start : start + rows].astype(F32) for ref in vectors for start in range(0, ref.shape[1], rows)
    ]
    index = lax.broadcasted_iota(jnp.int32, (VEC_LANES, rows), 0)
    table = jnp.zeros((VEC_LANES, rows), F32)
    for place, line in enumerate(lines):
        table = jnp.where(index == place, line, table)
    up_own[:, D:] = table.T.astype(BF16)


def run_quarter(up, qkv, vectors, rep):
    rows = up.shape[0]
    return pl.pallas_call(
        quarter_kernel,
        in_specs=[pl.BlockSpec(memory_space=pltpu.VMEM)] * (2 + len(vectors)) + [smem()],
        out_shape=[
            jax.ShapeDtypeStruct((rows, D + VEC_LANES), BF16),
            jax.ShapeDtypeStruct((rows, 3 * QUART), BF16),
        ],
        compiler_params=PARAMS,
        name="quarter",
    )(*vectors, up, qkv, rep)


def make_body(shards):
    bits = shards.bit_length() - 1
    rows = D // shards
    lowest_first = [1 << k for k in range(bits)]
    highest_first = lowest_first[::-1]

    def reverse(value, width):
        return sum(((value >> k) & 1) << (width - 1 - k) for k in range(width))

    def shard_swap(value, mask):
        return lax.ppermute(value, "fsdp", [(i, i ^ mask) for i in range(shards)])

    def core_swap(value):
        return lax.ppermute(value, "rep", [(i, i ^ 1) for i in range(GROUP)])

    def x_swap(value):
        return lax.ppermute(value, "rep", [(i, i ^ 2) for i in range(GROUP)])

    down_order = highest_first if rows % 16 else lowest_first[:1] + highest_first[:-1]
    down_place = [
        reverse(sum(mask for k, mask in enumerate(down_order) if (p >> k) & 1), bits) for p in range(shards)
    ]

    def gather_all(own, order=highest_first):
        for mask in order[:-1]:
            own = jnp.concatenate([own, shard_swap(own, mask)], axis=0)
        return own, shard_swap(own, order[-1])

    def add(keep, received):
        return keep.astype(F32) + received.astype(F32)

    def reduce_all(keep, send, order=lowest_first):
        for mask in order:
            total = add(keep, shard_swap(send, mask)).astype(BF16)
            half = total.shape[0] // 2
            keep, send = total[:half], total[half:]
        return total

    def body(
        block_input,
        segment_ids,
        out_cotangent,
        first_gain,
        first_shift,
        second_gain,
        second_shift,
        qkv_weight,
        qkv_bias,
        proj_weight,
        proj_bias,
        up_weight,
        up_bias,
        down_weight,
        down_bias,
    ):
        micro, slot = block_input.shape[0], block_input.shape[1]
        own_tokens = micro * slot
        mine = lax.axis_index("fsdp")
        rep = lax.axis_index("rep")
        core = rep % 2
        across = rep // 2
        top = mine // (shards // 4)
        top_across, top_core = top // 2, top % 2

        rep_ref = rep.reshape(1)
        vectors_own = [
            value.reshape(1, -1)
            for value in (
                first_gain, first_shift, second_gain, second_shift, qkv_bias, proj_bias, up_bias, down_bias
            )
        ]
        if rows % 32:
            vector_own = jnp.concatenate([value.reshape(-1, rows) for value in vectors_own], axis=0)
            vector_own = jnp.pad(vector_own, ((0, VEC_LANES - 13), (0, 0))).T
            up_own = lax.dynamic_index_in_dim(
                up_weight.reshape(rows, shards, GROUP, rows), rep, axis=2, keepdims=False
            ).reshape(rows, D)
            up_own = jnp.concatenate([up_own, vector_own], axis=1)
            qkv_own = lax.dynamic_index_in_dim(
                qkv_weight.reshape(rows, 3, GROUP, QUART), rep, axis=2, keepdims=False
            ).reshape(rows, 3 * QUART)
        else:
            up_own, qkv_own = run_quarter(up_weight, qkv_weight, vectors_own, rep_ref)
        down_own = lax.dynamic_index_in_dim(
            down_weight.reshape(GROUP, rows, D), rep, axis=0, keepdims=False
        )

        live = (segment_ids.reshape(own_tokens, 1) >= 0).astype(F32)
        own_input = block_input.reshape(own_tokens, D)
        own_grad = (out_cotangent.reshape(own_tokens, D).astype(F32) * live).astype(BF16)
        segment_row = jnp.pad(
            segment_ids.reshape(1, own_tokens).astype(BF16), ((0, 15), (0, D - own_tokens))
        )
        token_pack = jnp.concatenate([own_input, own_grad, segment_row], axis=0)
        token_across = x_swap(token_pack)
        token_beside = core_swap(token_pack)
        token_far = core_swap(token_across)
        packs = (token_pack, token_across, token_beside, token_far)

        up_lo, up_hi = gather_all(up_own)
        down_lo, down_hi = gather_all(down_own)
        qkv_lo, qkv_hi = gather_all(qkv_own)

        proj_part = jnp.where(top_across == across, proj_weight, shard_swap(proj_weight, highest_first[0]))
        proj_part = jnp.where(top_core == core, proj_part, shard_swap(proj_part, highest_first[1]))
        for mask in highest_first[2:]:
            proj_part = jnp.concatenate([proj_part, shard_swap(proj_part, mask)], axis=0)

        width = 3 * QUART
        block = np.array([reverse(p, bits) for p in range(shards)], np.int32)
        inner = np.arange(rows, dtype=np.int32)
        feature_block, feature_inner = np.repeat(block, rows), np.tile(inner, shards)
        natural = ((feature_block ^ mine) * rows + feature_inner)[None]
        low_block = np.array([reverse(p, bits - 2) for p in range(shards // 4)], np.int32)
        low_block, low_inner = np.repeat(low_block, rows), np.tile(inner, shards // 4)
        head_natural = ((low_block ^ (mine % (shards // 4))) * rows + low_inner)[None]
        shift = np.repeat(np.arange(3, dtype=np.int32) * rows, D)
        found = (np.tile(feature_block, 3) ^ mine) * (3 * rows) + (shift + np.tile(feature_inner, 3))
        found = jnp.where(found % D // QUART == rep, found // D * QUART + found % QUART, -1)[None]

        keep, send, pre, act, values, cotangents, vectors, up_rel, to_rel = run_mlp_forward(
            packs, up_lo, up_hi, natural, rep_ref, down_place
        )
        down_grad = reduce_all(keep, send, down_order[::-1])
        keep, send, mlp_part, mlp_norm, mlp_sums = run_mlp_backward(
            cotangents, down_lo, down_hi, up_rel, to_rel, pre, act, values, vectors
        )
        up_grad = reduce_all(keep, send)
        pair = jnp.concatenate([down_grad, up_grad], axis=1)
        keep, send, partial, partial_far = run_attention(
            cotangents, qkv_lo, qkv_hi, proj_part, to_rel, vectors, mlp_sums, found, head_natural,
            mlp_part, mlp_norm, values, rep_ref, rows,
        )

        side = width + VEC_LANES
        for mask in lowest_first[:-2]:
            total = add(keep, shard_swap(send, mask)).astype(BF16)
            half = total.shape[0] // 2
            keep, send = total[:half], total[half:]
        columns, proj_block = total[:, :side], total[:, side:]
        proj_block = jnp.concatenate([proj_block[: 2 * rows], proj_block[2 * rows :]], axis=1)
        packed = jnp.concatenate([columns[2 * rows :], proj_block], axis=1)
        sent = shard_swap(packed, lowest_first[-2])
        columns = add(columns[: 2 * rows], sent[:, :side])
        proj_block = add(proj_block, sent[:, side:])
        proj_block = jnp.concatenate(
            [
                proj_block[:rows, :QUART],
                proj_block[rows:, :QUART],
                proj_block[:rows, QUART:],
                proj_block[rows:, QUART:],
            ],
            axis=1,
        ).astype(BF16)
        packed = jnp.concatenate([columns[rows:].astype(BF16), proj_block], axis=1)
        own = jnp.concatenate([columns[:rows].astype(BF16), proj_block], axis=1)
        column = add(own, shard_swap(packed, lowest_first[-1])).astype(BF16)

        summed = add(partial, core_swap(partial_far))
        received = x_swap(summed[1].astype(BF16))
        block_out, input_grad = run_finish(token_pack, summed[0], received, to_rel, vectors, live)

        pair_across = x_swap(pair)
        pair_all = (pair, pair_across, core_swap(pair), core_swap(pair_across))
        column_across = x_swap(column)
        column_all = (column, column_across, core_swap(column), core_swap(column_across))
        where = jnp.stack([rep, top])
        up_out, down_out = (assemble_mlp_plain if rows % 32 else run_assemble_mlp)(pair_all, where, rows)
        qkv_out, proj_out, *vec = (assemble_plain if rows % 32 else run_assemble)(column_all, where, rows)
        vec = [each.reshape(-1) for each in vec]
        return (
            block_out.reshape(micro, slot, D),
            input_grad.reshape(micro, slot, D),
            vec[0],
            vec[1],
            vec[2],
            vec[3],
            qkv_out,
            vec[4],
            proj_out,
            vec[5],
            up_out,
            vec[6],
            down_out,
            vec[5],
        )

    return body


def solution(mesh):
    in_specs = (
        P(None, ("fsdp", "rep"), None),
        P(None, ("fsdp", "rep")),
        P(None, ("fsdp", "rep"), None),
        P("fsdp"),
        P("fsdp"),
        P("fsdp"),
        P("fsdp"),
        P("fsdp", None),
        P("fsdp"),
        P("fsdp", None),
        P("fsdp"),
        P("fsdp", None),
        P("fsdp"),
        P("fsdp", None),
        P("fsdp"),
    )
    out_specs = (
        P(None, ("fsdp", "rep"), None),
        P(None, ("fsdp", "rep"), None),
        P("fsdp"),
        P("fsdp"),
        P("fsdp"),
        P("fsdp"),
        P("fsdp", None),
        P("fsdp"),
        P("fsdp", None),
        P("fsdp"),
        P("fsdp", None),
        P("fsdp"),
        P("fsdp", None),
        P("fsdp"),
    )
    plain = make_body(mesh.shape["fsdp"])

    return jax.shard_map(plain, mesh=mesh, in_specs=in_specs, out_specs=out_specs, check_vma=False)
```

```python
import functools

import jax
import jax.numpy as jnp
import numpy as np
from jax import lax
from jax.experimental import pallas as pl
from jax.experimental.pallas import tpu as pltpu
from jax.sharding import PartitionSpec as P


D = 768
HEADS = 12
HDIM = 64
ROT = 16
FF = 3072
GROUP = 4
QUART = D // GROUP
LOCAL_HEADS = HEADS // GROUP
VEC_LANES = 128

EPSILON = 1e-05
NEG_FILL = -1e30
BF16 = jnp.bfloat16
F32 = jnp.float32


def dot(left, right):
    return jnp.dot(left, right, preferred_element_type=F32)


def dot_t(left, right):
    return lax.dot_general(left, right, (((1,), (1,)), ((), ())), preferred_element_type=F32)


def t_dot(left, right):
    return lax.dot_general(left, right, (((0,), (0,)), ((), ())), preferred_element_type=F32)


LANES = 128
EXT = LOCAL_HEADS * LANES


def layer_norm(values, gain_a, shift_a):
    centered = values - jnp.mean(values, axis=-1, keepdims=True)
    variance = jnp.mean(centered * centered, axis=-1, keepdims=True)
    inverse = lax.rsqrt(variance + EPSILON)
    unit = centered * inverse
    return (unit * gain_a + shift_a).astype(BF16), unit


def take(step, refs, rows):
    value = refs[-1][rows]
    for place in range(len(refs) - 2, -1, -1):
        value = jnp.where(step == place, refs[place][rows], value)
    return value


def hot(rows, columns):
    return jnp.where(rows == columns, 1.0, 0.0).astype(BF16)


def mlp_forward_kernel(
    down_place,
    near, across, beside, far, up_lo, up_hi, natural, rep,
    keep, send, slope_out, act_out, unit_out, grad_out_ref, vectors_out, up_rel, to_rel,
    down_acc,
):
    step = pl.program_id(0)
    packs = (near, across, beside, far)
    own = (near.shape[0] - 16) // 2
    half = D // 2

    @pl.when(step == 0)
    def _():
        to_rel[...] = hot(lax.broadcasted_iota(jnp.int32, (D, D), 0), natural[...])
        up_rel[:half] = dot(up_lo[:, :D], to_rel[...]).astype(BF16)
        up_rel[half:] = dot(up_hi[:, :D], to_rel[...]).astype(BF16)
        vectors_out[:, :half] = up_lo[:, D:].astype(F32).T[:16]
        vectors_out[:, half:] = up_hi[:, D:].astype(F32).T[:16]
        down_acc[...] = jnp.zeros_like(down_acc)

    inputs = take(step, packs, slice(0, own))
    rest = take(step, packs, slice(own, 2 * own + 16))
    grad_out_ref[0] = rest
    grad_out = rest[:own]
    normed, unit = layer_norm(dot(inputs, to_rel[...]), vectors_out[2:3], vectors_out[3:4])
    unit_out[0] = unit
    bias = vectors_out[11:12]
    for quarter in range(GROUP - 1):
        bias = jnp.where(rep[0] == quarter, vectors_out[8 + quarter : 9 + quarter], bias)
    pre_act = dot(normed, up_rel[...]) + bias
    phi = 0.5 * (1.0 + lax.erf(pre_act * 0.7071067811865476))
    activ = (pre_act * phi).astype(BF16)
    slope_out[0] = phi + pre_act * jnp.exp(-0.5 * pre_act * pre_act) * 0.3989422804014327
    act_out[0] = activ
    down_acc[...] += t_dot(activ, grad_out)

    @pl.when(step == pl.num_programs(0) - 1)
    def _():
        if down_place == sorted(down_place):
            keep[...] = down_acc[:half].astype(BF16)
            send[...] = down_acc[half:].astype(BF16)
        else:
            block = D // len(down_place)
            for target, source in enumerate(down_place):
                piece = send if target * block >= half else keep
                start = target * block % half
                piece[start : start + block] = down_acc[source * block : (source + 1) * block].astype(BF16)


def mlp_backward_kernel(
    cotangents, down_lo, down_hi, up_rel, to_rel, slope, act, unit_ref, vectors,
    keep, send, out_part, grad_norm, sums,
    down_rel, up_acc,
):
    step = pl.program_id(0)
    half = D // 2

    @pl.when(step == 0)
    def _():
        down_rel[:half] = down_lo[...]
        down_rel[half:] = down_hi[...]
        up_acc[...] = jnp.zeros_like(up_acc)
        sums[...] = jnp.zeros_like(sums)

    unit = unit_ref[0]
    grad_out = cotangents[0, : unit.shape[0]]
    normed = (unit * vectors[2:3] + vectors[3:4]).astype(BF16)
    grad_pre = dot_t(grad_out, down_rel[...]) * slope[0]
    grad_pre_b = grad_pre.astype(BF16)
    up_acc[...] += t_dot(normed, grad_pre_b)
    gn = dot_t(grad_pre_b, up_rel[...])
    out_part[0] = dot(act[0], down_rel[...])
    grad_norm[0] = gn
    sums[0:1] += jnp.sum(gn * unit, axis=0, keepdims=True)
    sums[1:2] += jnp.sum(gn, axis=0, keepdims=True)
    sums[2:3] += jnp.sum(grad_pre, axis=0, keepdims=True)

    @pl.when(step == pl.num_programs(0) - 1)
    def _():
        keep[...] = dot_t(up_acc[:half].astype(BF16), to_rel[...]).astype(BF16)
        send[...] = dot_t(up_acc[half:].astype(BF16), to_rel[...]).astype(BF16)


def attention_kernel(
    block_rows,
    cotangents, qkv_lo, qkv_hi, proj, to_rel, vectors, mlp_sums, found, source, head_natural,
    cosines, sines, mlp_part, mlp_norm, values, rep,
    keep, send, partial_near, partial_far,
    wide, proj_wide, bias_wide, qkv_rel, qkv_acc, proj_acc, gp_ref, ctx_ref, sums, bias_sums, place, spread, head_spread,
):
    step = pl.program_id(0)
    half = D // 2
    own = cotangents.shape[1] - 16

    @pl.when(step == 0)
    def _():
        width = 3 * QUART
        place[...] = hot(lax.broadcasted_iota(jnp.int32, (width, 3 * D), 0), found[...])
        spread[...] = hot(lax.broadcasted_iota(jnp.int32, (width, 3 * EXT), 0), source[...])
        padded = lax.broadcasted_iota(jnp.int32, (EXT, QUART), 0)
        padded = jnp.where(padded % LANES < HDIM, padded // LANES * HDIM + padded % LANES, -1)
        head_spread[...] = hot(padded, head_natural[...])
        qkv_rel[:half] = qkv_lo[...]
        qkv_rel[half:] = qkv_hi[...]
        wide[:half] = dot(qkv_lo[...], spread[...]).astype(BF16)
        wide[half:] = dot(qkv_hi[...], spread[...]).astype(BF16)
        proj_wide[...] = dot(head_spread[...], proj[...]).astype(BF16)
        vectors_b = vectors[...].astype(BF16)
        bias = sum(dot_t(vectors_b[4 + k : 5 + k], place[:, k * D : (k + 1) * D]) for k in range(3))
        bias = jnp.broadcast_to(bias, (8, bias.shape[1])).astype(BF16)
        bias_wide[...] = dot(bias, spread[...])
        qkv_acc[...] = jnp.zeros_like(qkv_acc)
        proj_acc[...] = jnp.zeros_like(proj_acc)
        sums[...] = jnp.zeros_like(sums)
        bias_sums[...] = jnp.zeros_like(bias_sums)

    grad_out = cotangents[0, :own]
    segment_row = cotangents[0, own:].astype(F32)
    unit = values[0]
    normed = (unit * vectors[0:1] + vectors[1:2]).astype(BF16)
    projected = dot(normed, wide[...]) + bias_wide[0:1]
    grad_context = dot_t(grad_out, proj_wide[...]).astype(BF16)
    lane = lax.broadcasted_iota(jnp.int32, (LANES, LANES), 1)
    sublane = lax.broadcasted_iota(jnp.int32, (LANES, LANES), 0)
    lower = lane < HDIM
    units = [(slab, head) for slab in range(own // LANES) for head in range(LOCAL_HEADS)]
    allowed, cos, sin = [], [], []
    for slab in range(own // LANES):
        seg_keys = jnp.broadcast_to(segment_row[0:1, slab * LANES : (slab + 1) * LANES], (LANES, LANES))
        same = seg_keys == seg_keys.T
        allowed.append(same & (lane <= sublane))
        position = jnp.sum(jnp.where(same & (lane < sublane), 1.0, 0.0), axis=1, keepdims=True)
        pick = (lane.astype(F32) == position).astype(BF16)
        cos.append(dot(pick, cosines[0]) + dot(pick, cosines[1]) + dot(pick, cosines[2]))
        sin.append(dot(pick, sines[0]) + dot(pick, sines[1]) + dot(pick, sines[2]))

    def part(value, unit, which):
        slab, head = unit
        start = which * EXT + head * LANES
        return value[slab * LANES : (slab + 1) * LANES, start : start + LANES]

    def turn(value, slab, direction):
        return value * cos[slab] + direction * (pltpu.roll(value, HDIM, 1) * sin[slab])

    query = [(turn(part(projected, u, 0), u[0], 1.0) * 0.125).astype(BF16) for u in units]
    key = [turn(part(projected, u, 1), u[0], 1.0).astype(BF16) for u in units]
    value = [part(projected, u, 2).astype(BF16) for u in units]
    gctx = [part(grad_context, u, 0) for u in units]
    count = range(len(units))
    scores = [dot_t(jnp.where(lower, query[n], jnp.zeros_like(query[n])), key[n]) for n in count]
    grad_probs = [dot_t(gctx[n], value[n]) for n in count]
    scores = [jnp.where(allowed[units[n][0]], scores[n], NEG_FILL) for n in count]
    weight = [jnp.exp(score - jnp.max(score, axis=-1, keepdims=True)) for score in scores]
    probs = [each * (1.0 / jnp.sum(each, axis=-1, keepdims=True)) for each in weight]
    probs_b = [each.astype(BF16) for each in probs]
    context = [dot(probs_b[n], value[n]) for n in count]
    grad_value = [t_dot(probs_b[n], gctx[n]) for n in count]
    delta = [jnp.sum(probs[n] * grad_probs[n], axis=-1, keepdims=True) for n in count]
    grad_sc = [(probs[n] * (grad_probs[n] - delta[n])).astype(BF16) for n in count]
    grad_query = [dot(grad_sc[n], key[n]) for n in count]
    grad_key = [t_dot(grad_sc[n], query[n]) for n in count]
    for n, (slab, head) in enumerate(units):
        row = slice(slab * LANES, (slab + 1) * LANES)
        ctx_ref[row, head * LANES : (head + 1) * LANES] = context[n].astype(BF16)
        turned = (
            turn(grad_query[n] * 0.125, slab, -1.0),
            turn(grad_key[n], slab, -1.0),
            grad_value[n],
        )
        for which, grad in enumerate(turned):
            start = which * QUART + head * HDIM
            gp_ref[row, start : start + HDIM] = grad[:, :HDIM]

    grad_proj = gp_ref[...]
    bias_sums[0:1] += jnp.sum(grad_proj, axis=0, keepdims=True)
    grad_proj = grad_proj.astype(BF16)
    qkv_acc[...] += t_dot(normed, grad_proj)
    gn = dot_t(grad_proj, qkv_rel[...])
    context = ctx_ref[...]
    proj_acc[...] += t_dot(dot(context, head_spread[...]).astype(BF16), grad_out)
    out_part = (dot(context, proj_wide[...]) + mlp_part[0]).astype(BF16)
    mixed = (gn * vectors[0:1] + mlp_norm[0] * vectors[2:3]).astype(BF16)
    sums[0:1] += jnp.sum(gn * unit, axis=0, keepdims=True)
    sums[1:2] += jnp.sum(gn, axis=0, keepdims=True)

    @pl.when(step < 2)
    def _():
        partial_near[0, :, :D] = out_part
        partial_near[0, :, D:] = mixed

    @pl.when(step >= 2)
    def _():
        partial_far[0, :, :D] = out_part
        partial_far[0, :, D:] = mixed

    @pl.when(step == 0)
    def _():
        sums[2:3] = jnp.sum(grad_out.astype(F32), axis=0, keepdims=True)

    @pl.when(step == pl.num_programs(0) - 1)
    def _():
        width = 3 * QUART
        side = width + VEC_LANES
        vec = lax.broadcasted_iota(jnp.int32, (VEC_LANES, D), 0)
        out_bias = dot(sums[...].astype(BF16), to_rel[...])[2:3]
        small = dot(bias_sums[...].astype(BF16), place[...])
        rows = [sums[0:1], sums[1:2], mlp_sums[0:1], mlp_sums[1:2]]
        rows += [small[0:1, k * D : (k + 1) * D] for k in range(3)] + [out_bias]
        table = jnp.where(vec == 8 + rep[0], mlp_sums[2:3], 0.0)
        for index, line in enumerate(rows):
            table = jnp.where(vec == index, line, table)
        table = table.T.astype(BF16)
        keep[:, :width] = qkv_acc[:half].astype(BF16)
        send[:, :width] = qkv_acc[half:].astype(BF16)
        keep[:, width:side] = table[:half]
        send[:, width:side] = table[half:]
        for target, first in ((keep, 0), (send, QUART // 2)):
            piece = proj_acc[first : first + QUART // 2]
            block = min(block_rows, QUART // 2)
            for start in range(0, QUART // 2, block):
                for quarter in range(GROUP):
                    target[
                        start * GROUP + quarter * block : start * GROUP + (quarter + 1) * block, side:
                    ] = piece[start : start + block, quarter * QUART : (quarter + 1) * QUART].astype(BF16)


def whole(*shape):
    return pl.BlockSpec(shape, lambda i: (0,) * len(shape))


def token_block(count, width):
    return pl.BlockSpec((1, count, width), lambda i: (i, 0, 0))


PARAMS = pltpu.CompilerParams(vmem_limit_bytes=60 * 1024 * 1024)


def smem():
    return pl.BlockSpec(memory_space=pltpu.SMEM)


def run_mlp_forward(packs, up_lo, up_hi, natural, rep, down_place):
    packed = packs[0].shape[0]
    own = (packed - 16) // 2
    half = D // 2
    wide = D + VEC_LANES
    grad = jax.ShapeDtypeStruct((half, D), BF16)
    return pl.pallas_call(
        functools.partial(mlp_forward_kernel, down_place),
        grid=(GROUP,),
        in_specs=[whole(packed, D)] * 4 + [whole(half, wide), whole(half, wide), whole(1, D), smem()],
        out_specs=[whole(half, D)] * 2
        + [token_block(own, D)] * 3
        + [token_block(own + 16, D), whole(16, D), whole(D, D), whole(D, D)],
        out_shape=[
            grad,
            grad,
            jax.ShapeDtypeStruct((GROUP, own, D), F32),
            jax.ShapeDtypeStruct((GROUP, own, D), BF16),
            jax.ShapeDtypeStruct((GROUP, own, D), F32),
            jax.ShapeDtypeStruct((GROUP, own + 16, D), BF16),
            jax.ShapeDtypeStruct((16, D), F32),
            jax.ShapeDtypeStruct((D, D), BF16),
            jax.ShapeDtypeStruct((D, D), BF16),
        ],
        scratch_shapes=[pltpu.VMEM((D, D), F32)],
        compiler_params=PARAMS,
        name="mlp_forward",
    )(*packs, up_lo, up_hi, natural, rep)


def run_mlp_backward(cotangents, down_lo, down_hi, up_rel, to_rel, pre, act, values, vectors):
    own = cotangents.shape[1] - 16
    half = D // 2
    grad = jax.ShapeDtypeStruct((half, D), BF16)
    acts = jax.ShapeDtypeStruct((GROUP, own, D), F32)
    return pl.pallas_call(
        mlp_backward_kernel,
        grid=(GROUP,),
        in_specs=[token_block(own + 16, D), whole(half, D), whole(half, D), whole(D, D), whole(D, D)]
        + [token_block(own, D)] * 3
        + [whole(16, D)],
        out_specs=[whole(half, D)] * 2 + [token_block(own, D)] * 2 + [whole(8, D)],
        out_shape=[grad, grad, acts, acts, jax.ShapeDtypeStruct((8, D), F32)],
        scratch_shapes=[pltpu.VMEM((D, D), BF16), pltpu.VMEM((D, D), F32)],
        compiler_params=PARAMS,
        name="mlp_backward",
    )(cotangents, down_lo, down_hi, up_rel, to_rel, pre, act, values, vectors)


def run_attention(cotangents, qkv_lo, qkv_hi, proj, to_rel, vectors, mlp_sums, found, head_natural, mlp_part, mlp_norm, values, rep, rows):
    own = cotangents.shape[1] - 16
    half = D // 2
    width = 3 * QUART
    column = np.arange(3 * EXT)
    which, head, unit = column // EXT, column % EXT // LANES, column % LANES
    inner = unit % HDIM
    halfway = ROT // 2
    partner = np.where(inner < halfway, inner + halfway, np.where(inner < ROT, inner - halfway, inner))
    source = which * QUART + head * HDIM + np.where(unit < HDIM, inner, partner)
    source = np.where((which == 2) & (unit >= HDIM), -1, source)
    source = jnp.asarray(source[None, :], jnp.int32)
    lane = np.arange(LANES) % HDIM
    angle = np.arange(LANES)[:, None] * (10000.0 ** (-(lane % halfway) / halfway))[None, :]
    sign = np.where(lane < halfway, -1.0, 1.0) * np.where(np.arange(LANES) < HDIM, 1.0, -1.0)
    turning = (lane < ROT)[None, :]
    tables = []
    for table in (np.where(turning, np.cos(angle), 1.0), np.where(turning, np.sin(angle) * sign, 0.0)):
        left = table.astype(np.float32)
        pieces = []
        for _ in range(3):
            piece = left.astype(BF16)
            pieces.append(piece)
            left = left - piece.astype(np.float32)
        tables.append(jnp.asarray(np.stack(pieces)))
    total = width + VEC_LANES + QUART
    grad = jax.ShapeDtypeStruct((half, total), BF16)
    part = jax.ShapeDtypeStruct((2, own, 2 * D), BF16)
    return pl.pallas_call(
        functools.partial(attention_kernel, rows),
        grid=(GROUP,),
        in_specs=[
            token_block(own + 16, D),
            whole(half, width),
            whole(half, width),
            whole(QUART, D),
            whole(D, D),
            whole(16, D),
            whole(8, D),
            whole(1, 3 * D),
            whole(1, 3 * EXT),
            whole(1, QUART),
            whole(3, LANES, LANES),
            whole(3, LANES, LANES),
            token_block(own, D),
            token_block(own, D),
            token_block(own, D),
            smem(),
        ],
        out_specs=[
            whole(half, total),
            whole(half, total),
            pl.BlockSpec((1, own, 2 * D), lambda i: (jnp.minimum(i, 1), 0, 0)),
            pl.BlockSpec((1, own, 2 * D), lambda i: (jnp.maximum(i - 2, 0), 0, 0)),
        ],
        out_shape=[grad, grad, part, part],
        scratch_shapes=[
            pltpu.VMEM((D, 3 * EXT), BF16),
            pltpu.VMEM((EXT, D), BF16),
            pltpu.VMEM((8, 3 * EXT), F32),
            pltpu.VMEM((D, width), BF16),
            pltpu.VMEM((D, width), F32),
            pltpu.VMEM((QUART, D), F32),
            pltpu.VMEM((own, width), F32),
            pltpu.VMEM((own, EXT), BF16),
            pltpu.VMEM((8, D), F32),
            pltpu.VMEM((8, width), F32),
            pltpu.VMEM((width, 3 * D), BF16),
            pltpu.VMEM((width, 3 * EXT), BF16),
            pltpu.VMEM((EXT, QUART), BF16),
        ],
        compiler_params=PARAMS,
        name="attention",
    )(
        cotangents, qkv_lo, qkv_hi, proj, to_rel, vectors, mlp_sums, found, source, head_natural, *tables, mlp_part, mlp_norm,
        values, rep
    )


def finish_kernel(pack, near, received, to_rel, vectors, live, block_out, input_grad):
    vectors_nat = dot_t(vectors[...].astype(BF16), to_rel[...])
    out_bias = vectors_nat[7:8] + vectors_nat[12:13]
    own = near.shape[0]
    partial = near[...].astype(F32) + received[...].astype(F32)
    block_out[...] = (live[...] * (pack[:own].astype(F32) + partial[:, :D] + out_bias)).astype(BF16)
    values = dot(pack[:own], to_rel[...])
    centered = values - jnp.mean(values, axis=-1, keepdims=True)
    inverse = lax.rsqrt(jnp.mean(centered * centered, axis=-1, keepdims=True) + EPSILON)
    unit = centered * inverse
    error = partial[:, D:]
    through = inverse * (
        error
        - jnp.mean(error, axis=-1, keepdims=True)
        - unit * jnp.mean(error * unit, axis=-1, keepdims=True)
    )
    grad = (dot(pack[own : 2 * own], to_rel[...]) + through).astype(BF16)
    input_grad[...] = dot_t(grad, to_rel[...]).astype(BF16)


def run_finish(pack, near, received, to_rel, vectors, live):
    own = near.shape[0]
    out = jax.ShapeDtypeStruct((own, D), BF16)
    return pl.pallas_call(finish_kernel, out_shape=[out, out], compiler_params=PARAMS, name="finish")(
        pack, near, received, to_rel, vectors, live
    )


def owner(values, rep, natural):
    first, second, third, fourth = values
    chosen = jnp.where(rep == natural ^ 1, third, fourth)
    chosen = jnp.where(rep == natural ^ 2, second, chosen)
    return jnp.where(rep == natural, first, chosen)


def assemble_mlp_kernel(*refs):
    pairs, rep, up_out, down_out = refs[:4], refs[4][0], refs[5], refs[6]
    rows = up_out.shape[0]
    for natural in range(GROUP):
        down_out[natural * rows : (natural + 1) * rows] = owner([ref[:, :D].astype(F32) for ref in pairs], rep, natural)
        up = owner([ref[:, D:].astype(F32) for ref in pairs], rep, natural)
        for shard in range(D // rows):
            start = (shard * GROUP + natural) * rows
            up_out[:, start : start + rows] = up[:, shard * rows : (shard + 1) * rows]


def run_assemble_mlp(pairs, place, rows):
    return pl.pallas_call(
        assemble_mlp_kernel,
        in_specs=[pl.BlockSpec(memory_space=pltpu.VMEM)] * 4 + [smem()],
        out_shape=[jax.ShapeDtypeStruct((rows, FF), F32), jax.ShapeDtypeStruct((GROUP * rows, D), F32)],
        compiler_params=PARAMS,
        name="assemble_mlp",
    )(*pairs, place)


def assemble_mlp_plain(pairs, place, rows):
    swapped = jnp.arange(GROUP) ^ place[0]
    pairs_nat = jnp.stack(pairs).astype(F32)[(swapped % 2) * 2 + swapped // 2]
    up = pairs_nat[:, :, D:].reshape(GROUP, rows, D // rows, rows).transpose(1, 2, 0, 3)
    return up.reshape(rows, FF), pairs_nat[:, :, :D].reshape(GROUP * rows, D)


VEC_PARTS = (1, 1, 1, 1, 3, 1, GROUP, 1)
VEC_LINES = (0, 1, 2, 3, 4, 7, 8, 7)


def assemble_kernel(*refs):
    columns, place = refs[:4], refs[4]
    qkv_out, proj_out, vec_outs = refs[5], refs[6], refs[7:]
    rows = proj_out.shape[0]
    width = 3 * QUART
    side = width + VEC_LANES
    rep, top = place[0], place[1]
    for natural in range(GROUP):
        qkv = owner([ref[:, :width].astype(F32) for ref in columns], rep, natural)
        for which in range(3):
            start = (which * GROUP + natural) * QUART
            qkv_out[:, start : start + QUART] = qkv[:, which * QUART : (which + 1) * QUART]
    proj_out[...] = owner([ref[:, side:].astype(F32) for ref in columns], rep, top)
    vec = [ref[:, width:side].astype(F32) for ref in columns]
    vec = ((vec[0] + vec[1]) + (vec[2] + vec[3])).T[:16]
    for out, line in zip(vec_outs, VEC_LINES):
        count = out.shape[0] // rows
        out[...] = jnp.concatenate([vec[line + k : line + k + 1] for k in range(count)], axis=1).reshape(out.shape)


def run_assemble(columns, place, rows):
    shapes = [(rows, 3 * D), (rows, D)] + [(count * rows,) for count in VEC_PARTS]
    return pl.pallas_call(
        assemble_kernel,
        in_specs=[pl.BlockSpec(memory_space=pltpu.VMEM)] * 4 + [smem()],
        out_shape=[jax.ShapeDtypeStruct(shape, F32) for shape in shapes],
        compiler_params=PARAMS,
        name="assemble",
    )(*columns, place)


def assemble_plain(columns, place, rows):
    width = 3 * QUART
    side = width + VEC_LANES
    columns = jnp.stack(columns).astype(F32)
    swapped = jnp.arange(GROUP) ^ place[0]
    columns_nat = columns[(swapped % 2) * 2 + swapped // 2]
    qkv = columns_nat[:, :, :width].reshape(GROUP, rows, 3, QUART).transpose(1, 2, 0, 3)
    vec = columns[:, :, width:side]
    vec = ((vec[0] + vec[1]) + (vec[2] + vec[3])).T
    outs = [vec[line : line + count].reshape(-1) for line, count in zip(VEC_LINES, VEC_PARTS)]
    return (qkv.reshape(rows, 3 * D), columns_nat[place[1]][:, side:], *outs)


def quarter_kernel(*refs):
    vectors, (up, qkv, rep, up_own, qkv_own) = refs[:-5], refs[-5:]
    rows = up.shape[0]
    for natural in range(GROUP):

        @pl.when(rep[0] == natural)
        def _():
            for shard in range(D // rows):
                start = (shard * GROUP + natural) * rows
                up_own[:, shard * rows : (shard + 1) * rows] = up[:, start : start + rows]
            for which in range(3):
                start = (which * GROUP + natural) * QUART
                qkv_own[:, which * QUART : (which + 1) * QUART] = qkv[:, start : start + QUART]

    lines = [
        ref[...].astype(F32).reshape(1, ref.shape[0])[:, start : start + rows]
        for ref in vectors
        for start in range(0, ref.shape[0], rows)
    ]
    index = lax.broadcasted_iota(jnp.int32, (VEC_LANES, rows), 0)
    table = jnp.zeros((VEC_LANES, rows), F32)
    for place, line in enumerate(lines):
        table = jnp.where(index == place, line, table)
    up_own[:, D:] = table.T.astype(BF16)


def run_quarter(up, qkv, vectors, rep):
    rows = up.shape[0]
    return pl.pallas_call(
        quarter_kernel,
        in_specs=[pl.BlockSpec(memory_space=pltpu.VMEM)] * (2 + len(vectors)) + [smem()],
        out_shape=[
            jax.ShapeDtypeStruct((rows, D + VEC_LANES), BF16),
            jax.ShapeDtypeStruct((rows, 3 * QUART), BF16),
        ],
        compiler_params=PARAMS,
        name="quarter",
    )(*vectors, up, qkv, rep)


def make_body(shards):
    bits = shards.bit_length() - 1
    rows = D // shards
    lowest_first = [1 << k for k in range(bits)]
    highest_first = lowest_first[::-1]

    def reverse(value, width):
        return sum(((value >> k) & 1) << (width - 1 - k) for k in range(width))

    def shard_swap(value, mask):
        return lax.ppermute(value, "fsdp", [(i, i ^ mask) for i in range(shards)])

    def core_swap(value):
        return lax.ppermute(value, "rep", [(i, i ^ 1) for i in range(GROUP)])

    def x_swap(value):
        return lax.ppermute(value, "rep", [(i, i ^ 2) for i in range(GROUP)])

    down_order = highest_first if rows % 16 else lowest_first[:1] + highest_first[:-1]
    down_place = [
        reverse(sum(mask for k, mask in enumerate(down_order) if (p >> k) & 1), bits) for p in range(shards)
    ]

    def gather_all(own, order=highest_first):
        for mask in order[:-1]:
            own = jnp.concatenate([own, shard_swap(own, mask)], axis=0)
        return own, shard_swap(own, order[-1])

    def add(keep, received):
        return keep.astype(F32) + received.astype(F32)

    def reduce_all(keep, send, order=lowest_first):
        for mask in order:
            total = add(keep, shard_swap(send, mask)).astype(BF16)
            half = total.shape[0] // 2
            keep, send = total[:half], total[half:]
        return total

    def body(
        block_input,
        segment_ids,
        out_cotangent,
        first_gain,
        first_shift,
        second_gain,
        second_shift,
        qkv_weight,
        qkv_bias,
        proj_weight,
        proj_bias,
        up_weight,
        up_bias,
        down_weight,
        down_bias,
    ):
        micro, slot = block_input.shape[0], block_input.shape[1]
        own_tokens = micro * slot
        mine = lax.axis_index("fsdp")
        rep = lax.axis_index("rep")
        core = rep % 2
        across = rep // 2
        top = mine // (shards // 4)
        top_across, top_core = top // 2, top % 2

        rep_ref = rep.reshape(1)
        vectors_own = [
            value
            for value in (
                first_gain, first_shift, second_gain, second_shift, qkv_bias, proj_bias, up_bias, down_bias
            )
        ]
        if rows % 32:
            vector_own = jnp.concatenate([value.reshape(-1, rows) for value in vectors_own], axis=0)
            vector_own = jnp.pad(vector_own, ((0, VEC_LANES - 13), (0, 0))).T
            up_own = lax.dynamic_index_in_dim(
                up_weight.reshape(rows, shards, GROUP, rows), rep, axis=2, keepdims=False
            ).reshape(rows, D)
            up_own = jnp.concatenate([up_own, vector_own], axis=1)
            qkv_own = lax.dynamic_index_in_dim(
                qkv_weight.reshape(rows, 3, GROUP, QUART), rep, axis=2, keepdims=False
            ).reshape(rows, 3 * QUART)
        else:
            up_own, qkv_own = run_quarter(up_weight, qkv_weight, vectors_own, rep_ref)
        down_own = lax.dynamic_index_in_dim(
            down_weight.reshape(GROUP, rows, D), rep, axis=0, keepdims=False
        )

        live = (segment_ids.reshape(own_tokens, 1) >= 0).astype(F32)
        own_input = block_input.reshape(own_tokens, D)
        own_grad = (out_cotangent.reshape(own_tokens, D).astype(F32) * live).astype(BF16)
        segment_row = jnp.pad(
            segment_ids.reshape(1, own_tokens).astype(BF16), ((0, 15), (0, D - own_tokens))
        )
        token_pack = jnp.concatenate([own_input, own_grad, segment_row], axis=0)
        token_across = x_swap(token_pack)
        token_beside = core_swap(token_pack)
        token_far = core_swap(token_across)
        packs = (token_pack, token_across, token_beside, token_far)

        up_lo, up_hi = gather_all(up_own)
        down_lo, down_hi = gather_all(down_own)
        qkv_lo, qkv_hi = gather_all(qkv_own)

        proj_part = jnp.where(top_across == across, proj_weight, shard_swap(proj_weight, highest_first[0]))
        proj_part = jnp.where(top_core == core, proj_part, shard_swap(proj_part, highest_first[1]))
        for mask in highest_first[2:]:
            proj_part = jnp.concatenate([proj_part, shard_swap(proj_part, mask)], axis=0)

        width = 3 * QUART
        block = np.array([reverse(p, bits) for p in range(shards)], np.int32)
        inner = np.arange(rows, dtype=np.int32)
        feature_block, feature_inner = np.repeat(block, rows), np.tile(inner, shards)
        natural = ((feature_block ^ mine) * rows + feature_inner)[None]
        low_block = np.array([reverse(p, bits - 2) for p in range(shards // 4)], np.int32)
        low_block, low_inner = np.repeat(low_block, rows), np.tile(inner, shards // 4)
        head_natural = ((low_block ^ (mine % (shards // 4))) * rows + low_inner)[None]
        shift = np.repeat(np.arange(3, dtype=np.int32) * rows, D)
        found = (np.tile(feature_block, 3) ^ mine) * (3 * rows) + (shift + np.tile(feature_inner, 3))
        found = jnp.where(found % D // QUART == rep, found // D * QUART + found % QUART, -1)[None]

        keep, send, pre, act, values, cotangents, vectors, up_rel, to_rel = run_mlp_forward(
            packs, up_lo, up_hi, natural, rep_ref, down_place
        )
        down_grad = reduce_all(keep, send, down_order[::-1])
        keep, send, mlp_part, mlp_norm, mlp_sums = run_mlp_backward(
            cotangents, down_lo, down_hi, up_rel, to_rel, pre, act, values, vectors
        )
        up_grad = reduce_all(keep, send)
        pair = jnp.concatenate([down_grad, up_grad], axis=1)
        keep, send, partial, partial_far = run_attention(
            cotangents, qkv_lo, qkv_hi, proj_part, to_rel, vectors, mlp_sums, found, head_natural,
            mlp_part, mlp_norm, values, rep_ref, rows,
        )

        side = width + VEC_LANES
        for mask in lowest_first[:-2]:
            total = add(keep, shard_swap(send, mask)).astype(BF16)
            half = total.shape[0] // 2
            keep, send = total[:half], total[half:]
        columns, proj_block = total[:, :side], total[:, side:]
        proj_block = jnp.concatenate([proj_block[: 2 * rows], proj_block[2 * rows :]], axis=1)
        packed = jnp.concatenate([columns[2 * rows :], proj_block], axis=1)
        sent = shard_swap(packed, lowest_first[-2])
        columns = add(columns[: 2 * rows], sent[:, :side])
        proj_block = add(proj_block, sent[:, side:])
        proj_block = jnp.concatenate(
            [
                proj_block[:rows, :QUART],
                proj_block[rows:, :QUART],
                proj_block[:rows, QUART:],
                proj_block[rows:, QUART:],
            ],
            axis=1,
        ).astype(BF16)
        packed = jnp.concatenate([columns[rows:].astype(BF16), proj_block], axis=1)
        own = jnp.concatenate([columns[:rows].astype(BF16), proj_block], axis=1)
        column = add(own, shard_swap(packed, lowest_first[-1])).astype(BF16)

        summed = add(partial, core_swap(partial_far))
        received = x_swap(summed[1].astype(BF16))
        block_out, input_grad = run_finish(token_pack, summed[0], received, to_rel, vectors, live)

        pair_across = x_swap(pair)
        pair_all = (pair, pair_across, core_swap(pair), core_swap(pair_across))
        column_across = x_swap(column)
        column_all = (column, column_across, core_swap(column), core_swap(column_across))
        where = jnp.stack([rep, top])
        up_out, down_out = (assemble_mlp_plain if rows % 32 else run_assemble_mlp)(pair_all, where, rows)
        qkv_out, proj_out, *vec = (assemble_plain if rows % 32 else run_assemble)(column_all, where, rows)
        return (
            block_out.reshape(micro, slot, D),
            input_grad.reshape(micro, slot, D),
            vec[0],
            vec[1],
            vec[2],
            vec[3],
            qkv_out,
            vec[4],
            proj_out,
            vec[5],
            up_out,
            vec[6],
            down_out,
            vec[7],
        )

    return body


def solution(mesh):
    in_specs = (
        P(None, ("fsdp", "rep"), None),
        P(None, ("fsdp", "rep")),
        P(None, ("fsdp", "rep"), None),
        P("fsdp"),
        P("fsdp"),
        P("fsdp"),
        P("fsdp"),
        P("fsdp", None),
        P("fsdp"),
        P("fsdp", None),
        P("fsdp"),
        P("fsdp", None),
        P("fsdp"),
        P("fsdp", None),
        P("fsdp"),
    )
    out_specs = (
        P(None, ("fsdp", "rep"), None),
        P(None, ("fsdp", "rep"), None),
        P("fsdp"),
        P("fsdp"),
        P("fsdp"),
        P("fsdp"),
        P("fsdp", None),
        P("fsdp"),
        P("fsdp", None),
        P("fsdp"),
        P("fsdp", None),
        P("fsdp"),
        P("fsdp", None),
        P("fsdp"),
    )
    plain = make_body(mesh.shape["fsdp"])

    return jax.shard_map(plain, mesh=mesh, in_specs=in_specs, out_specs=out_specs, check_vma=False)
```
